32 devices in a mesh: modes: 16 (over z, x, core), gz: 2 (over y).
Axes of the slice: x: 2, y: 2, z: 4, core: 2. Of those that a mesh axis runs over, the one named last changes fastest.
Arguments:
- launch_spectrum: float32 [2, 256, 16384], P(None, 'modes'), may hold values from -6 to 6
- step_phase: float32 [256, 16384], P('modes'), may hold values from -3.140625 to 3.140625
- mode_profiles: bfloat16 [2048, 256], replicated, may hold values from -0.375 to 0.375
- kerr_weights: float32 [2048], replicated, may hold values from 0.02 to 0.2
Outputs:
- spectra: float32 [2, 2, 256, 16384], P('gz', None, 'modes')
The draws below stay inside these ranges and needn't reach their ends.
All inputs are finite; a program needn't handle non-finite values.
Results may differ from the reference program's by a relative error of at most 0.0025.
Values may be sent and summed in bfloat16 or wider, within the bound.
No kernel may reach another device: no remote copies, remote signals or barrier semaphores. Data moves between devices by JAX's collectives and lax.ppermute only.
A program may use at most 64 MiB of HBM per device.

```python
import math
import jax
import jax.numpy as jnp
from jax import lax

M = 256
T_SIZE = 16384
P_SIZE = 2048
ZDEV = 1
ITERS = 1
N_GZ = 2


def shard_levels(rng, extent, shards, low, top_value):
    level = 1.0
    for axis_at, shards_of in shards:
        steps = jax.random.uniform(jax.random.fold_in(jax.random.fold_in(rng, 6), axis_at), (shards_of,), jnp.float32, low / len(shards), top_value / len(shards))
        level = level * jnp.repeat(jnp.exp(steps), extent[axis_at] // shards_of).reshape((-1,) + (1,) * (len(extent) - 1 - axis_at))
    return level


def gaussian(rng, dims, width, reach, shards=(), dtype=jnp.bfloat16):
    values = width * jax.random.normal(rng, dims, jnp.float32)
    if shards:
        values = values * shard_levels(rng, dims, shards, -0.22, 0.18)
    return jnp.clip(values, -reach, reach).astype(dtype)


def setup_inputs(seed: int = 0) -> dict:
    keys = jax.random.split(jax.random.key(seed), 5)
    launch_spectrum = gaussian(keys[0], (2, M, T_SIZE), 1.0, 6.0, ((1, 16),), jnp.float32)
    step_phase = jnp.clip(jax.random.uniform(keys[1], (M, T_SIZE), jnp.float32, -3.140625, 3.140625), -3.140625, 3.140625)
    mode_profiles = gaussian(keys[2], (P_SIZE, M), M ** -0.5, 0.375)
    kerr_weights = jnp.clip(jnp.exp(jax.random.uniform(keys[3], (P_SIZE,), jnp.float32, math.log(0.02), math.log(0.2))), 0.02, 0.2)
    return dict(launch_spectrum=launch_spectrum, step_phase=step_phase, mode_profiles=mode_profiles, kerr_weights=kerr_weights)


def point_increment(spectrum_now, point_factor, launch_spectrum, step_phase, mode_profiles, kerr_weights):
    phase = step_phase * point_factor
    cosine = jnp.cos(phase)
    sine_part = jnp.sin(phase)
    rotated_real = spectrum_now[0] * cosine - spectrum_now[1] * sine_part
    rotated_imag = spectrum_now[0] * sine_part + spectrum_now[1] * cosine
    pulses = jnp.fft.ifft(lax.complex(rotated_real, rotated_imag), axis=-1, norm="ortho")
    fields = jnp.stack([jnp.real(pulses), jnp.imag(pulses)]).astype(jnp.bfloat16)
    profiles = mode_profiles.astype(jnp.float32)
    expanded = jnp.einsum("pm,cmt->cpt", profiles, fields.astype(jnp.float32))
    power = expanded[0:1] * expanded[0:1] + expanded[1:2] * expanded[1:2]
    cubed = (kerr_weights[None, :, None] * power * expanded).astype(jnp.bfloat16)
    projected = jnp.einsum("pm,cpt->cmt", profiles, cubed.astype(jnp.float32)).astype(jnp.bfloat16)
    projected = projected.astype(jnp.float32)
    turned = jnp.fft.fft(lax.complex(-projected[1], projected[0]), axis=-1, norm="ortho")
    spec_real = jnp.real(turned)
    spec_imag = jnp.imag(turned)
    inc_real = spec_real * cosine + spec_imag * sine_part
    inc_imag = spec_imag * cosine - spec_real * sine_part
    return jnp.stack([inc_real, inc_imag])


def reference(launch_spectrum, step_phase, mode_profiles, kerr_weights):
    points = ZDEV * N_GZ
    spectra = jnp.broadcast_to(launch_spectrum[None], (points,) + launch_spectrum.shape)
    factors = jnp.arange(1, points + 1).astype(jnp.float32)
    for repeat in range(ITERS):
        def one_point(packed):
            return point_increment(packed[0], packed[1], launch_spectrum, step_phase, mode_profiles, kerr_weights)

        increments = lax.map(one_point, (spectra, factors))
        spectra = launch_spectrum[None] + jnp.cumsum(increments, axis=0)
    return spectra
```

```python
import functools
import math

import jax
import jax.numpy as jnp
import numpy as np
from jax import lax
from jax.experimental import pallas as pl
from jax.experimental.pallas import tpu as pltpu
from jax.sharding import PartitionSpec as P

RADIX = 128
CHUNKS = 2
VMEM = pltpu.MemorySpace.VMEM
SMEM = pltpu.MemorySpace.SMEM

f32 = jnp.float32
bf16 = jnp.bfloat16


def halves(table):
    high = table.astype(jnp.bfloat16)
    low = (table - high.astype(np.float64)).astype(jnp.bfloat16)
    return high, low


@functools.lru_cache(None)
def tables(length):
    radix = RADIX
    other = length // radix
    index = np.arange(radix)
    second = np.arange(other)
    scale = 1.0 / math.sqrt(length)
    angle = 2.0 * math.pi / radix * (index[:, None] * index[None, :] % radix)
    cos, sin = np.cos(angle), np.sin(angle)
    last = 2.0 * math.pi / other * (second[:, None] * second[None, :] % other)
    cos2, sin2 = np.cos(last), np.sin(last)
    turn = 2.0 * math.pi / length * (index[:, None] * second[None, :] % length)
    twist = np.stack([np.cos(turn), np.sin(turn)]).astype(np.float32)
    inv_first = np.block([[cos, -sin], [sin, cos]])
    inv_second = np.block([[cos2, sin2], [-sin2, cos2]]) * scale
    fwd_first = np.block([[sin2, cos2], [-cos2, sin2]])
    fwd_second = np.block([[cos, sin], [-sin, cos]]) * scale
    return dict(
        twist=twist,
        inv_first=halves(inv_first),
        inv_second=halves(inv_second),
        fwd_first=halves(fwd_first),
        fwd_second=halves(fwd_second),
    )


def split(values):
    high = values.astype(bf16)
    return high, (values - high.astype(f32)).astype(bf16)


def dot(left, right):
    return lax.dot_general(left, right, (((1,), (0,)), ((), ())), preferred_element_type=f32)


TWO_PI = 2.0 * math.pi
TWO_PI_HIGH = float(np.float32(6.28125))
TWO_PI_LOW = TWO_PI - TWO_PI_HIGH
SIN_TERMS = [(-1) ** n / math.factorial(2 * n + 1) for n in range(6)]
COS_TERMS = [(-1) ** n / math.factorial(2 * n) for n in range(7)]


def sincos(phase):
    turns = jnp.round(phase * (1.0 / TWO_PI))
    rest = (phase - turns * TWO_PI_HIGH) - turns * TWO_PI_LOW
    half = 0.5 * rest
    square = half * half
    sine = SIN_TERMS[-1]
    for term in SIN_TERMS[-2::-1]:
        sine = sine * square + term
    sine = sine * half
    cosine = COS_TERMS[-1]
    for term in COS_TERMS[-2::-1]:
        cosine = cosine * square + term
    twice = sine + sine
    return twice * cosine, 1.0 - twice * sine


def inverse_kernel(modes, devices, chunks, factor, launch, phase, twist, fh, fl, sh, sl, *rest):
    outs, (natural, turned) = rest[:chunks], rest[chunks:]
    radix = RADIX

    def rotate(k1, carry):
        at = pl.ds(pl.multiple_of(k1 * radix, radix), radix)
        rows = pl.ds(pl.multiple_of(k1 * modes, modes), modes)
        sine, cosine = sincos(phase[:, at] * factor[0, 0])
        real, imag = launch[0, :, at], launch[1, :, at]
        natural[0, rows, :] = real * cosine - imag * sine
        natural[1, rows, :] = real * sine + imag * cosine
        return carry

    lax.fori_loop(0, radix, rotate, 0, unroll=4)
    for pair in range(modes // 2):
        both = []
        for m in (2 * pair, 2 * pair + 1):
            both.append(
                jnp.concatenate([natural[c, pl.ds(m, radix, stride=modes), :] for c in range(2)], 0)
            )
        high, low = split(jnp.concatenate(both, 1))
        section = dot(fh[...], high) + (dot(fh[...], low) + dot(fl[...], high))
        rows = []
        for side in range(2):
            real = section[:radix, side * radix : (side + 1) * radix]
            imag = section[radix:, side * radix : (side + 1) * radix]
            rows.append(
                jnp.concatenate(
                    [real * twist[0] - imag * twist[1], real * twist[1] + imag * twist[0]], 1
                )
            )
        high, low = split(jnp.concatenate(rows, 0))
        final = dot(high, sh[...]) + (dot(low, sh[...]) + dot(high, sl[...]))
        for side in range(2):
            for c in range(2):
                turned[c, pl.ds(2 * pair + side, radix, stride=modes), :] = final[
                    side * radix : (side + 1) * radix, c * radix : (c + 1) * radix
                ]
    each = radix // chunks // devices
    for t2 in range(radix):
        chunk, rest_at = divmod(t2, radix // chunks)
        target, slot = divmod(rest_at, each)
        for c in range(2):
            outs[chunk][target, c * modes : (c + 1) * modes, slot * radix : (slot + 1) * radix] = (
                turned[c, t2 * modes : (t2 + 1) * modes, :].astype(bf16)
            )


def specs(count, scalars=1):
    return [pl.BlockSpec(memory_space=SMEM)] * scalars + [pl.BlockSpec(memory_space=VMEM)] * count


def params():
    return pltpu.CompilerParams(vmem_limit_bytes=48 * 1024 * 1024)


def inverse(factor, launch, phase, devices, chunks):
    _, modes, length = launch.shape
    if not regular(modes):
        return inverse_plain(factor, launch, phase, devices, chunks)
    table = tables(length)
    width = length // devices // chunks
    shape = jax.ShapeDtypeStruct((devices, 2 * modes, width), bf16)
    return pl.pallas_call(
        functools.partial(inverse_kernel, modes, devices, chunks),
        out_shape=[shape] * chunks,
        in_specs=specs(7),
        out_specs=[pl.BlockSpec(memory_space=VMEM)] * chunks,
        scratch_shapes=[pltpu.VMEM((2, RADIX * modes, RADIX), f32)] * 2,
        compiler_params=params(),
        name="inverse",
    )(factor, launch, phase, table["twist"], *table["inv_first"], *table["inv_second"])


def kerr_kernel(modes, devices, step, fields, profiles, flipped, weights, out, gathered, total):
    points = profiles.shape[0]
    every = devices * modes
    for c in range(2):
        for source in range(devices):
            gathered[c, source * modes : (source + 1) * modes, :] = fields[
                source, c * modes : (c + 1) * modes, :
            ]
    sums = None
    for at in range(0, points, step):
        lines = profiles[at : at + step, :]
        real = dot(lines, gathered[0])
        imag = dot(lines, gathered[1])
        power = weights[at : at + step, :] * (real * real + imag * imag)
        back = flipped[:, at : at + step]
        parts = [dot(back, (power * real).astype(bf16)), dot(back, (power * imag).astype(bf16))]
        if at == 0:
            total[0], total[1] = parts
        else:
            total[0] += parts[0]
            total[1] += parts[1]
    for c in range(2):
        for target in range(devices):
            out[target, c * modes : (c + 1) * modes, :] = total[
                c, target * modes : (target + 1) * modes, :
            ].astype(bf16)


def kerr(fields, profiles, flipped, weights, modes):
    devices, _, width = fields.shape
    if not regular(modes):
        return kerr_plain(fields, profiles, weights, modes)
    return pl.pallas_call(
        functools.partial(kerr_kernel, modes, devices, 256),
        out_shape=jax.ShapeDtypeStruct(fields.shape, bf16),
        in_specs=specs(4, 0),
        out_specs=pl.BlockSpec(memory_space=VMEM),
        scratch_shapes=[
            pltpu.VMEM((2, devices * modes, width), bf16),
            pltpu.VMEM((2, devices * modes, width), f32),
        ],
        compiler_params=params(),
        name="kerr",
    )(fields, profiles, flipped, weights)


def forward_kernel(modes, devices, chunks, factor, base, phase, twist, fh, fl, sh, sl, *rest):
    ins, out, (turned, final) = rest[:chunks], rest[chunks], rest[chunks + 1 :]
    radix = RADIX
    each = radix // chunks // devices
    t2 = 0
    for chunk in range(chunks):
        for source in range(devices):
            rows = []
            for slot in range(each):
                at = slice(slot * radix, (slot + 1) * radix)
                rows.append(
                    jnp.concatenate(
                        [ins[chunk][source, c * modes : (c + 1) * modes, at] for c in range(2)], 1
                    )
                )
            block = jnp.concatenate(rows, 0)
            section = dot(block, fh[...]) + dot(block, fl[...])
            for slot in range(each):
                here = slice(slot * modes, (slot + 1) * modes)
                real, imag = section[here, :radix], section[here, radix:]
                cosine, sine = twist[0, t2 : t2 + 1, :], twist[1, t2 : t2 + 1, :]
                turned[0, t2 * modes : (t2 + 1) * modes, :] = real * cosine + imag * sine
                turned[1, t2 * modes : (t2 + 1) * modes, :] = imag * cosine - real * sine
                t2 += 1
    for pair in range(modes // 2):
        both = []
        for m in (2 * pair, 2 * pair + 1):
            both.append(
                jnp.concatenate([turned[c, pl.ds(m, radix, stride=modes), :] for c in range(2)], 0)
            )
        high, low = split(jnp.concatenate(both, 1))
        section = dot(sh[...], high) + (dot(sh[...], low) + dot(sl[...], high))
        for side in range(2):
            for c in range(2):
                final[c, pl.ds(2 * pair + side, radix, stride=modes), :] = section[
                    c * radix : (c + 1) * radix, side * radix : (side + 1) * radix
                ]

    def finish(k1, carry):
        at = pl.ds(pl.multiple_of(k1 * radix, radix), radix)
        rows = pl.ds(pl.multiple_of(k1 * modes, modes), modes)
        sine, cosine = sincos(phase[:, at] * factor[0, 0])
        real, imag = final[0, rows, :], final[1, rows, :]
        out[0, :, at] = base[0, :, at] + (real * cosine + imag * sine)
        out[1, :, at] = base[1, :, at] + (imag * cosine - real * sine)
        return carry

    lax.fori_loop(0, radix, finish, 0, unroll=4)


def forward(factor, base, phase, pieces, devices):
    _, modes, length = base.shape
    if not regular(modes):
        return forward_plain(factor, base, phase, pieces, devices)
    table = tables(length)
    chunks = len(pieces)
    return pl.pallas_call(
        functools.partial(forward_kernel, modes, devices, chunks),
        out_shape=jax.ShapeDtypeStruct(base.shape, f32),
        in_specs=specs(7 + chunks),
        out_specs=pl.BlockSpec(memory_space=VMEM),
        scratch_shapes=[pltpu.VMEM((2, RADIX * modes, RADIX), f32)] * 2,
        compiler_params=params(),
        name="forward",
    )(factor, base, phase, table["twist"], *table["fwd_first"], *table["fwd_second"], *pieces)


def regular(modes):
    return modes % 16 == 0


def matrix(name, length):
    high, low = tables(length)[name]
    return high.astype(np.float32) + low.astype(np.float32)


def einsum(text, left, right):
    return jnp.einsum(text, left, right, precision=lax.Precision.HIGHEST)


def inverse_plain(factor, launch, phase, devices, chunks):
    _, modes, length = launch.shape
    twist = tables(length)["twist"]
    angle = phase * factor[0, 0]
    cosine, sine = jnp.cos(angle), jnp.sin(angle)
    real = launch[0] * cosine - launch[1] * sine
    imag = launch[0] * sine + launch[1] * cosine
    both = jnp.stack([real, imag]).reshape(2, modes, RADIX, -1)
    first = matrix("inv_first", length).reshape(2, RADIX, 2, RADIX)
    real, imag = einsum("dtck,cmkj->dmtj", first, both)
    both = jnp.stack([real * twist[0] - imag * twist[1], real * twist[1] + imag * twist[0]])
    other = length // RADIX
    second = matrix("inv_second", length).reshape(2, other, 2, other)
    both = einsum("cmtj,cjdu->dmtu", both, second).astype(bf16)
    both = both.reshape(2, modes, chunks, devices, -1)
    pieces = both.transpose(2, 3, 0, 1, 4).reshape(chunks, devices, 2 * modes, -1)
    return [pieces[chunk] for chunk in range(chunks)]


def kerr_plain(fields, profiles, weights, modes):
    devices, _, width = fields.shape
    fields = fields.reshape(devices, 2, modes, width).swapaxes(0, 1)
    fields = fields.reshape(2, devices * modes, width)
    expanded = jnp.einsum("pm,cmt->cpt", profiles, fields, preferred_element_type=f32)
    power = weights * (expanded[0] * expanded[0] + expanded[1] * expanded[1])
    cubed = (power * expanded).astype(bf16)
    projected = jnp.einsum("pm,cpt->cmt", profiles, cubed, preferred_element_type=f32)
    projected = projected.astype(bf16).reshape(2, devices, modes, width)
    return projected.swapaxes(0, 1).reshape(devices, 2 * modes, width)


def forward_plain(factor, base, phase, pieces, devices):
    _, modes, length = base.shape
    other = length // RADIX
    twist = tables(length)["twist"]
    both = jnp.stack(pieces).astype(f32).reshape(len(pieces), devices, 2, modes, -1, other)
    both = both.transpose(2, 3, 0, 1, 4, 5).reshape(2, modes, RADIX, other)
    first = matrix("fwd_first", length).reshape(2, other, 2, other)
    real, imag = einsum("cmtu,cudj->dmtj", both, first)
    both = jnp.stack([real * twist[0] + imag * twist[1], imag * twist[0] - real * twist[1]])
    second = matrix("fwd_second", length).reshape(2, RADIX, 2, RADIX)
    real, imag = einsum("dkct,cmtj->dmkj", second, both).reshape(2, modes, length)
    angle = phase * factor[0, 0]
    cosine, sine = jnp.cos(angle), jnp.sin(angle)
    return base + jnp.stack([real * cosine + imag * sine, imag * cosine - real * sine])


def scalar(value):
    return value.astype(f32).reshape(1, 1)


def on_device(devices, points, launch, phase, profiles, weights):
    _, modes, length = launch.shape
    place = lax.axis_index("gz")
    pieces = inverse(scalar(place + 1), launch, phase, devices, CHUNKS)
    flipped = profiles.T
    wide = weights[:, None]
    exchange = functools.partial(
        lax.all_to_all, axis_name="modes", split_axis=0, concat_axis=0, tiled=True
    )
    pieces = [exchange(piece) for piece in pieces]
    pieces = [exchange(kerr(piece, profiles, flipped, wide, modes)) for piece in pieces]
    carried = []
    for shift in range(1, points):
        pairs = [(k, k + shift) for k in range(points - shift)]
        carried.append([lax.ppermute(piece, "gz", pairs) for piece in pieces])
    result = forward(scalar(place + 1), launch, phase, pieces, devices)
    for shift, held in enumerate(carried, 1):
        result = forward(scalar(place + 1 - shift), result, phase, held, devices)
    return result[None]


def solution(mesh):
    in_specs = (P(None, "modes", None), P("modes", None), P(), P())
    out_specs = P("gz", None, "modes", None)
    body = functools.partial(on_device, mesh.shape["modes"], mesh.shape["gz"])
    return jax.shard_map(body, mesh=mesh, in_specs=in_specs, out_specs=out_specs, check_vma=False)
```

```python
import functools
import math

import jax
import jax.numpy as jnp
import numpy as np
from jax import lax
from jax.experimental import pallas as pl
from jax.experimental.pallas import tpu as pltpu
from jax.sharding import PartitionSpec as P

RADIX = 128
STRIPES = 8
SPACES = pltpu.MemorySpace

f32 = jnp.float32
bf16 = jnp.bfloat16


def halves(table):
    high = table.astype(jnp.bfloat16)
    low = (table - high.astype(np.float64)).astype(jnp.bfloat16)
    return high, low


@functools.lru_cache(None)
def tables(length):
    radix = RADIX
    other = length // radix
    index = np.arange(radix)
    second = np.arange(other)
    scale = 1.0 / math.sqrt(length)
    angle = 2.0 * math.pi / radix * (index[:, None] * index[None, :] % radix)
    cos, sin = np.cos(angle), np.sin(angle)
    last = 2.0 * math.pi / other * (second[:, None] * second[None, :] % other)
    cos2, sin2 = np.cos(last), np.sin(last)
    turn = 2.0 * math.pi / length * (index[:, None] * second[None, :] % length)
    twist = np.stack([np.cos(turn), np.sin(turn)]).astype(np.float32)
    inv_first = np.block([[cos, -sin], [sin, cos]])
    inv_second = np.block([[cos2, sin2], [-sin2, cos2]]) * scale
    fwd_first = np.block([[sin2, cos2], [-cos2, sin2]])
    fwd_second = np.block([[cos, sin], [-sin, cos]]) * scale
    return dict(
        twist=twist,
        inv_first=halves(inv_first),
        inv_second=halves(inv_second),
        fwd_first=halves(fwd_first),
        fwd_second=halves(fwd_second),
    )


def split(values):
    high = values.astype(bf16)
    return high, (values - high.astype(f32)).astype(bf16)


def dot(left, right):
    return lax.dot_general(left, right, (((1,), (0,)), ((), ())), preferred_element_type=f32)


TWO_PI = 2.0 * math.pi
TWO_PI_HIGH = float(np.float32(6.28125))
TWO_PI_LOW = TWO_PI - TWO_PI_HIGH
SIN_TERMS = [(-1) ** n / math.factorial(2 * n + 1) for n in range(6)]
COS_TERMS = [(-1) ** n / math.factorial(2 * n) for n in range(7)]


def sincos(phase):
    turns = jnp.round(phase * (1.0 / TWO_PI))
    rest = (phase - turns * TWO_PI_HIGH) - turns * TWO_PI_LOW
    half = 0.5 * rest
    square = half * half
    sine = SIN_TERMS[-1]
    for term in SIN_TERMS[-2::-1]:
        sine = sine * square + term
    sine = sine * half
    cosine = COS_TERMS[-1]
    for term in COS_TERMS[-2::-1]:
        cosine = cosine * square + term
    twice = sine + sine
    return twice * cosine, 1.0 - twice * sine


def specs(text):
    spaces = dict(s=SPACES.SMEM, v=SPACES.VMEM, h=SPACES.HBM, a=pl.ANY)
    return [pl.BlockSpec(memory_space=spaces[letter]) for letter in text]


def params():
    return pltpu.CompilerParams(vmem_limit_bytes=48 * 1024 * 1024)


def stripe(at, length):
    width = length // STRIPES
    return slice(at * width, (at + 1) * width)


def inverse_kernel(
    modes,
    devices,
    factor,
    launch,
    phase,
    twist,
    fh,
    fl,
    sh,
    sl,
    out,
    natural,
    turned,
    launched,
    phases,
    sems,
):
    radix = RADIX
    length = launch.shape[-1]
    copies = []
    for at in range(STRIPES):
        cut = stripe(at, length)
        copies.append(
            [
                pltpu.make_async_copy(
                    launch.at[:, :, cut], launched.at[:, :, cut], sems.at[2 * at]
                ),
                pltpu.make_async_copy(phase.at[:, cut], phases.at[:, cut], sems.at[2 * at + 1]),
            ]
        )
        for copy in copies[-1]:
            copy.start()

    def rotate(k1, carry):
        at = pl.ds(pl.multiple_of(k1 * radix, radix), radix)
        rows = pl.ds(pl.multiple_of(k1 * modes, modes), modes)
        sine, cosine = sincos(phases[:, at] * factor[0, 0])
        real, imag = launched[0, :, at], launched[1, :, at]
        natural[0, rows, :] = real * cosine - imag * sine
        natural[1, rows, :] = real * sine + imag * cosine
        return carry

    for at in range(STRIPES):
        for copy in copies[at]:
            copy.wait()
        part = radix // STRIPES
        lax.fori_loop(at * part, (at + 1) * part, rotate, 0, unroll=4)
    for pair in range(modes // 2):
        both = []
        for m in (2 * pair, 2 * pair + 1):
            both.append(
                jnp.concatenate([natural[c, pl.ds(m, radix, stride=modes), :] for c in range(2)], 0)
            )
        high, low = split(jnp.concatenate(both, 1))
        section = dot(fh[...], high) + (dot(fh[...], low) + dot(fl[...], high))
        rows = []
        for side in range(2):
            real = section[:radix, side * radix : (side + 1) * radix]
            imag = section[radix:, side * radix : (side + 1) * radix]
            rows.append(
                jnp.concatenate(
                    [real * twist[0] - imag * twist[1], real * twist[1] + imag * twist[0]], 1
                )
            )
        high, low = split(jnp.concatenate(rows, 0))
        final = dot(high, sh[...]) + (dot(low, sh[...]) + dot(high, sl[...]))
        for side in range(2):
            for c in range(2):
                turned[c, pl.ds(2 * pair + side, radix, stride=modes), :] = final[
                    side * radix : (side + 1) * radix, c * radix : (c + 1) * radix
                ]
    each = radix // devices
    for t2 in range(radix):
        target, slot = divmod(t2, each)
        for c in range(2):
            out[target, c * modes : (c + 1) * modes, slot * radix : (slot + 1) * radix] = turned[
                c, t2 * modes : (t2 + 1) * modes, :
            ].astype(bf16)


def inverse(factor, launch, phase, devices):
    _, modes, length = launch.shape
    table = tables(length)
    return pl.pallas_call(
        functools.partial(inverse_kernel, modes, devices),
        out_shape=jax.ShapeDtypeStruct((devices, 2 * modes, length // devices), bf16),
        in_specs=specs("shhvvvvv"),
        out_specs=specs("v")[0],
        scratch_shapes=[
            pltpu.VMEM((2, RADIX * modes, RADIX), f32),
            pltpu.VMEM((2, RADIX * modes, RADIX), f32),
            pltpu.VMEM(launch.shape, f32),
            pltpu.VMEM(phase.shape, f32),
            pltpu.SemaphoreType.DMA((2 * STRIPES,)),
        ],
        compiler_params=params(),
        name="inverse",
    )(
        factor,
        *[
            pltpu.with_memory_space_constraint(value, SPACES.HBM)
            for value in (
                launch,
                phase,
                *map(jnp.asarray, (table["twist"], *table["inv_first"], *table["inv_second"])),
            )
        ],
    )


def kerr_kernel(modes, devices, step, me, fields, profiles, flipped, weights, *rest):
    outs, (gathered, total, sems) = rest[:devices], rest[devices:]
    points = profiles.shape[0]
    width = fields.shape[-1]
    tiles = 2
    lanes = width // tiles
    copies = []
    for tile in range(tiles):
        cut = slice(tile * lanes, (tile + 1) * lanes)
        for source in range(devices):
            for c in range(2):
                copies.append(
                    pltpu.make_async_copy(
                        fields.at[source, c * modes : (c + 1) * modes, cut],
                        gathered.at[c, source * modes : (source + 1) * modes, cut],
                        sems.at[len(copies)],
                    )
                )
                copies[-1].start()
    for tile in range(tiles):
        cut = slice(tile * lanes, (tile + 1) * lanes)
        for copy in copies[tile * 2 * devices : (tile + 1) * 2 * devices]:
            copy.wait()
        for at in range(0, points, step):
            lines = profiles[at : at + step, :]
            real = dot(lines, gathered[0, :, cut])
            imag = dot(lines, gathered[1, :, cut])
            power = weights[at : at + step, :] * (real * real + imag * imag)
            back = flipped[:, at : at + step]
            parts = [dot(back, (power * real).astype(bf16)), dot(back, (power * imag).astype(bf16))]
            if at == 0:
                total[0, :, cut], total[1, :, cut] = parts
            else:
                total[0, :, cut] += parts[0]
                total[1, :, cut] += parts[1]
    for hop in range(devices):
        rows = pl.ds(pl.multiple_of((me[0, 0] ^ hop) * modes, modes), modes)
        for c in range(2):
            outs[hop][c * modes : (c + 1) * modes, :] = total[c, rows, :].astype(bf16)


def kerr(me, fields, profiles, flipped, weights, modes):
    devices, _, width = fields.shape
    return pl.pallas_call(
        functools.partial(kerr_kernel, modes, devices, 512),
        out_shape=[jax.ShapeDtypeStruct((2 * modes, width), bf16)] * devices,
        in_specs=specs("savvv"),
        out_specs=specs("v" * devices),
        scratch_shapes=[
            pltpu.VMEM((2, devices * modes, width), bf16),
            pltpu.VMEM((2, devices * modes, width), f32),
            pltpu.SemaphoreType.DMA((4 * devices,)),
        ],
        compiler_params=params(),
        name="kerr",
    )(me, fields, profiles, flipped, weights)


def first_section(modes, block, source, each, twist, fh, fl, write):
    radix = RADIX
    rows = []
    for slot in range(each):
        at = slice(slot * radix, (slot + 1) * radix)
        rows.append(
            jnp.concatenate([block[c * modes : (c + 1) * modes, at] for c in range(2)], 1)
        )
    block = jnp.concatenate(rows, 0)
    section = dot(block, fh[...]) + dot(block, fl[...])
    for slot in range(each):
        here = slice(slot * modes, (slot + 1) * modes)
        real, imag = section[here, :radix], section[here, radix:]
        row = pl.ds(source * each + slot, 1)
        cosine, sine = twist[0, row, :], twist[1, row, :]
        write(0, slot, real * cosine + imag * sine)
        write(1, slot, imag * cosine - real * sine)


def late_kernel(modes, devices, last, me, factor, base, phase, twist, fh, fl, sh, sl, *rest):
    groups, out, (turned, final), spare = rest[:4], rest[4], rest[5:7], rest[7:]
    radix = RADIX
    each = radix // devices
    size = each * modes
    length = base.shape[-1]
    for group, hops in zip(groups, groups_of(devices)):
        for at, hop in enumerate(hops):
            source = me[0, 0] ^ hop

            def write(c, slot, values, source=source):
                rows = pl.ds(pl.multiple_of(source * size + slot * modes, modes), modes)
                turned[c, rows, :] = values

            first_section(modes, group.at[at], source, each, twist, fh, fl, write)
    for pair in range(modes // 2):
        both = []
        for m in (2 * pair, 2 * pair + 1):
            both.append(
                jnp.concatenate([turned[c, pl.ds(m, radix, stride=modes), :] for c in range(2)], 0)
            )
        high, low = split(jnp.concatenate(both, 1))
        section = dot(sh[...], high) + (dot(sh[...], low) + dot(sl[...], high))
        for side in range(2):
            for c in range(2):
                final[c, pl.ds(2 * pair + side, radix, stride=modes), :] = section[
                    c * radix : (c + 1) * radix, side * radix : (side + 1) * radix
                ]
    result = spare[0] if last else out

    def finish(k1, carry):
        at = pl.ds(pl.multiple_of(k1 * radix, radix), radix)
        rows = pl.ds(pl.multiple_of(k1 * modes, modes), modes)
        sine, cosine = sincos(phase[:, at] * factor[0, 0])
        real, imag = final[0, rows, :], final[1, rows, :]
        result[0, :, at] = base[0, :, at] + (real * cosine + imag * sine)
        result[1, :, at] = base[1, :, at] + (imag * cosine - real * sine)
        return carry

    copies = []
    for at in range(STRIPES):
        cut = stripe(at, length)
        part = radix // STRIPES
        lax.fori_loop(at * part, (at + 1) * part, finish, 0, unroll=4)
        if last:
            copies.append(
                pltpu.make_async_copy(result.at[:, :, cut], out.at[:, :, cut], spare[1].at[at])
            )
            copies[-1].start()
    for copy in copies:
        copy.wait()


def late(me, factor, groups, base, phase, devices, last):
    _, modes, length = base.shape
    table = tables(length)
    spare = [pltpu.VMEM(base.shape, f32), pltpu.SemaphoreType.DMA((STRIPES,))]
    return pl.pallas_call(
        functools.partial(late_kernel, modes, devices, last),
        out_shape=jax.ShapeDtypeStruct(base.shape, f32),
        in_specs=specs("ssvvvvvvvvvvv"),
        out_specs=specs("h" if last else "v")[0],
        scratch_shapes=[pltpu.VMEM((2, RADIX * modes, RADIX), f32)] * 2 + (spare if last else []),
        compiler_params=params(),
        name="late",
    )(
        me,
        factor,
        base,
        phase,
        table["twist"],
        *table["fwd_first"],
        *table["fwd_second"],
        *groups,
    )


def regular(modes, devices):
    return modes % 16 == 0 and devices & (devices - 1) == 0 and 4 <= devices <= RADIX


def matrix(name, length):
    high, low = tables(length)[name]
    return high.astype(np.float32) + low.astype(np.float32)


def einsum(text, left, right):
    return jnp.einsum(text, left, right, precision=lax.Precision.HIGHEST)


def inverse_plain(factor, launch, phase, devices):
    _, modes, length = launch.shape
    twist = tables(length)["twist"]
    angle = phase * factor[0, 0]
    cosine, sine = jnp.cos(angle), jnp.sin(angle)
    real = launch[0] * cosine - launch[1] * sine
    imag = launch[0] * sine + launch[1] * cosine
    both = jnp.stack([real, imag]).reshape(2, modes, RADIX, -1)
    first = matrix("inv_first", length).reshape(2, RADIX, 2, RADIX)
    real, imag = einsum("dtck,cmkj->dmtj", first, both)
    both = jnp.stack([real * twist[0] - imag * twist[1], real * twist[1] + imag * twist[0]])
    other = length // RADIX
    second = matrix("inv_second", length).reshape(2, other, 2, other)
    both = einsum("cmtj,cjdu->dmtu", both, second).astype(bf16)
    both = both.reshape(2, modes, devices, -1)
    return both.transpose(2, 0, 1, 3).reshape(devices, 2 * modes, -1)


def kerr_plain(fields, profiles, weights, modes):
    devices, _, width = fields.shape
    fields = fields.reshape(devices, 2, modes, width).swapaxes(0, 1)
    fields = fields.reshape(2, devices * modes, width)
    expanded = jnp.einsum("pm,cmt->cpt", profiles, fields, preferred_element_type=f32)
    power = weights * (expanded[0] * expanded[0] + expanded[1] * expanded[1])
    cubed = (power * expanded).astype(bf16)
    projected = jnp.einsum("pm,cpt->cmt", profiles, cubed, preferred_element_type=f32)
    projected = projected.astype(bf16).reshape(2, devices, modes, width)
    return projected.swapaxes(0, 1).reshape(devices, 2 * modes, width)


def forward_plain(factor, base, phase, piece, devices):
    _, modes, length = base.shape
    other = length // RADIX
    twist = tables(length)["twist"]
    both = piece.astype(f32).reshape(devices, 2, modes, -1, other)
    both = both.transpose(1, 2, 0, 3, 4).reshape(2, modes, RADIX, other)
    first = matrix("fwd_first", length).reshape(2, other, 2, other)
    real, imag = einsum("cmtu,cudj->dmtj", both, first)
    both = jnp.stack([real * twist[0] + imag * twist[1], imag * twist[0] - real * twist[1]])
    second = matrix("fwd_second", length).reshape(2, RADIX, 2, RADIX)
    real, imag = einsum("dkct,cmtj->dmkj", second, both).reshape(2, modes, length)
    angle = phase * factor[0, 0]
    cosine, sine = jnp.cos(angle), jnp.sin(angle)
    return base + jnp.stack([real * cosine + imag * sine, imag * cosine - real * sine])


def scalar(value, dtype=f32):
    return value.astype(dtype).reshape(1, 1)


def onward(values, points):
    held = []
    for shift in range(1, points):
        pairs = [(k, k + shift) for k in range(points - shift)]
        held.append(lax.ppermute(values, "gz", pairs))
    return held


def on_device_plain(devices, points, launch, phase, profiles, weights):
    _, modes, _ = launch.shape
    place = lax.axis_index("gz")
    exchange = functools.partial(
        lax.all_to_all, axis_name="modes", split_axis=0, concat_axis=0, tiled=True
    )
    piece = exchange(inverse_plain(scalar(place + 1), launch, phase, devices))
    piece = exchange(kerr_plain(piece, profiles, weights[:, None], modes))
    result = forward_plain(scalar(place + 1), launch, phase, piece, devices)
    for shift, held in enumerate(onward(piece, points), 1):
        result = forward_plain(scalar(place + 1 - shift), result, phase, held, devices)
    return result[None]


def groups_of(devices):
    part = devices // 4
    return [tuple(range(at * part, (at + 1) * part)) for at in range(4)]


def on_device(devices, points, launch, phase, profiles, weights):
    _, modes, _ = launch.shape
    if not regular(modes, devices):
        return on_device_plain(devices, points, launch, phase, profiles, weights)
    place = lax.axis_index("gz")
    me = lax.axis_index("modes")
    here = scalar(me, jnp.int32)
    fields = inverse(scalar(place + 1), launch, phase, devices)
    fields = lax.all_to_all(fields, "modes", 0, 0, tiled=True)
    sent = kerr(here, fields, profiles, profiles.T, weights[:, None], modes)
    got = [sent[0]]
    for hop in range(1, devices):
        pairs = [(a, a ^ hop) for a in range(devices)]
        got.append(lax.ppermute(sent[hop], "modes", pairs))
    groups = groups_of(devices)
    waiting = []
    for hops in groups:
        pieces = jnp.stack([got[hop] for hop in hops])
        waiting.append([pieces] + onward(pieces, points))
    result = launch
    for shift in range(points):
        result = late(
            here,
            scalar(place + 1 - shift),
            [held[shift] for held in waiting],
            result,
            phase,
            devices,
            shift == points - 1,
        )
    return result[None]


def solution(mesh):
    in_specs = (P(None, "modes", None), P("modes", None), P(), P())
    out_specs = P("gz", None, "modes", None)
    devices, points = mesh.shape["modes"], mesh.shape["gz"]
    body = functools.partial(on_device, devices, points)
    return jax.shard_map(body, mesh=mesh, in_specs=in_specs, out_specs=out_specs, check_vma=False)
```

```python
import functools
import math

import jax
import jax.numpy as jnp
import numpy as np
from jax import lax
from jax.experimental import pallas as pl
from jax.experimental.pallas import tpu as pltpu
from jax.sharding import PartitionSpec as P

RADIX = 128
STRIPES = 8
SPACES = pltpu.MemorySpace

f32 = jnp.float32
bf16 = jnp.bfloat16


def halves(table):
    high = table.astype(jnp.bfloat16)
    low = (table - high.astype(np.float64)).astype(jnp.bfloat16)
    return high, low


@functools.lru_cache(None)
def tables(length):
    radix = RADIX
    other = length // radix
    index = np.arange(radix)
    second = np.arange(other)
    scale = 1.0 / math.sqrt(length)
    angle = 2.0 * math.pi / radix * (index[:, None] * index[None, :] % radix)
    cos, sin = np.cos(angle), np.sin(angle)
    last = 2.0 * math.pi / other * (second[:, None] * second[None, :] % other)
    cos2, sin2 = np.cos(last), np.sin(last)
    turn = 2.0 * math.pi / length * (index[:, None] * second[None, :] % length)
    twist = np.stack([np.cos(turn), np.sin(turn)]).astype(np.float32)
    inv_first = np.block([[cos, -sin], [sin, cos]])
    inv_second = np.block([[cos2, sin2], [-sin2, cos2]]) * scale
    fwd_first = np.block([[sin2, cos2], [-cos2, sin2]])
    fwd_second = np.block([[cos, sin], [-sin, cos]]) * scale
    return dict(
        twist=twist,
        inv_first=halves(inv_first),
        inv_second=halves(inv_second),
        fwd_first=halves(fwd_first),
        fwd_second=halves(fwd_second),
    )


def split(values):
    high = values.astype(bf16)
    return high, (values - high.astype(f32)).astype(bf16)


def dot(left, right):
    return lax.dot_general(left, right, (((1,), (0,)), ((), ())), preferred_element_type=f32)


TWO_PI = 2.0 * math.pi
TWO_PI_HIGH = float(np.float32(6.28125))
TWO_PI_LOW = TWO_PI - TWO_PI_HIGH
SIN_TERMS = [(-1) ** n / math.factorial(2 * n + 1) for n in range(6)]
COS_TERMS = [(-1) ** n / math.factorial(2 * n) for n in range(7)]


def sincos(phase):
    turns = jnp.round(phase * (1.0 / TWO_PI))
    rest = (phase - turns * TWO_PI_HIGH) - turns * TWO_PI_LOW
    half = 0.5 * rest
    square = half * half
    sine = SIN_TERMS[-1]
    for term in SIN_TERMS[-2::-1]:
        sine = sine * square + term
    sine = sine * half
    cosine = COS_TERMS[-1]
    for term in COS_TERMS[-2::-1]:
        cosine = cosine * square + term
    twice = sine + sine
    return twice * cosine, 1.0 - twice * sine


def specs(text):
    spaces = dict(s=SPACES.SMEM, v=SPACES.VMEM, h=SPACES.HBM, a=pl.ANY)
    return [pl.BlockSpec(memory_space=spaces[letter]) for letter in text]


def params():
    return pltpu.CompilerParams(vmem_limit_bytes=48 * 1024 * 1024)


def stripe(at, length):
    width = length // STRIPES
    return slice(at * width, (at + 1) * width)


def inverse_kernel(
    modes,
    devices,
    factor,
    launch,
    phase,
    twist,
    fh,
    fl,
    sh,
    sl,
    out,
    natural,
    turned,
    launched,
    phases,
    sems,
):
    radix = RADIX
    length = launch.shape[-1]
    copies = []
    for at in range(STRIPES):
        cut = stripe(at, length)
        copies.append(
            [
                pltpu.make_async_copy(
                    launch.at[:, :, cut], launched.at[:, :, cut], sems.at[2 * at]
                ),
                pltpu.make_async_copy(phase.at[:, cut], phases.at[:, cut], sems.at[2 * at + 1]),
            ]
        )
        for copy in copies[-1]:
            copy.start()

    def rotate(k1, carry):
        at = pl.ds(pl.multiple_of(k1 * radix, radix), radix)
        rows = pl.ds(pl.multiple_of(k1 * modes, modes), modes)
        sine, cosine = sincos(phases[:, at] * factor[0, 0])
        real, imag = launched[0, :, at], launched[1, :, at]
        natural[0, rows, :] = real * cosine - imag * sine
        natural[1, rows, :] = real * sine + imag * cosine
        return carry

    for at in range(STRIPES):
        for copy in copies[at]:
            copy.wait()
        part = radix // STRIPES
        lax.fori_loop(at * part, (at + 1) * part, rotate, 0, unroll=4)
    for pair in range(modes // 2):
        both = []
        for m in (2 * pair, 2 * pair + 1):
            both.append(
                jnp.concatenate([natural[c, pl.ds(m, radix, stride=modes), :] for c in range(2)], 0)
            )
        high, low = split(jnp.concatenate(both, 1))
        section = dot(fh[...], high) + (dot(fh[...], low) + dot(fl[...], high))
        rows = []
        for side in range(2):
            real = section[:radix, side * radix : (side + 1) * radix]
            imag = section[radix:, side * radix : (side + 1) * radix]
            rows.append(
                jnp.concatenate(
                    [real * twist[0] - imag * twist[1], real * twist[1] + imag * twist[0]], 1
                )
            )
        high, low = split(jnp.concatenate(rows, 0))
        final = dot(high, sh[...]) + (dot(low, sh[...]) + dot(high, sl[...]))
        for side in range(2):
            for c in range(2):
                turned[c, pl.ds(2 * pair + side, radix, stride=modes), :] = final[
                    side * radix : (side + 1) * radix, c * radix : (c + 1) * radix
                ]
    each = radix // devices
    for t2 in range(radix):
        target, slot = divmod(t2, each)
        for c in range(2):
            out[target, c * modes : (c + 1) * modes, slot * radix : (slot + 1) * radix] = turned[
                c, t2 * modes : (t2 + 1) * modes, :
            ].astype(bf16)


def inverse(factor, launch, phase, devices):
    _, modes, length = launch.shape
    table = tables(length)
    return pl.pallas_call(
        functools.partial(inverse_kernel, modes, devices),
        out_shape=jax.ShapeDtypeStruct((devices, 2 * modes, length // devices), bf16),
        in_specs=specs("shhvvvvv"),
        out_specs=specs("v")[0],
        scratch_shapes=[
            pltpu.VMEM((2, RADIX * modes, RADIX), f32),
            pltpu.VMEM((2, RADIX * modes, RADIX), f32),
            pltpu.VMEM(launch.shape, f32),
            pltpu.VMEM(phase.shape, f32),
            pltpu.SemaphoreType.DMA((2 * STRIPES,)),
        ],
        compiler_params=params(),
        name="inverse",
    )(
        factor,
        *[
            pltpu.with_memory_space_constraint(value, SPACES.HBM)
            for value in (
                launch,
                phase,
                *map(jnp.asarray, (table["twist"], *table["inv_first"], *table["inv_second"])),
            )
        ],
    )


def kerr_kernel(modes, devices, step, me, fields, profiles, flipped, weights, *rest):
    chips = devices // 2
    keeps, gives, (gathered, total, spread, sems) = (
        rest[:chips],
        rest[chips : chips + 2],
        rest[-4:],
    )
    points = profiles.shape[0]
    width = fields.shape[-1]
    tiles = 4
    for at in range(points // RADIX):
        column = jnp.broadcast_to(weights[at : at + 1, :], (RADIX, RADIX)).T
        spread[at * RADIX : (at + 1) * RADIX, :] = column
    lanes = width // tiles
    copies = []
    for tile in range(tiles):
        cut = slice(tile * lanes, (tile + 1) * lanes)
        for source in range(devices):
            for c in range(2):
                copies.append(
                    pltpu.make_async_copy(
                        fields.at[source, c * modes : (c + 1) * modes, cut],
                        gathered.at[c, source * modes : (source + 1) * modes, cut],
                        sems.at[len(copies)],
                    )
                )
                copies[-1].start()
    for tile in range(tiles):
        cut = slice(tile * lanes, (tile + 1) * lanes)
        for copy in copies[tile * 2 * devices : (tile + 1) * 2 * devices]:
            copy.wait()
        for at in range(0, points, step):
            lines = profiles[at : at + step, :]
            real = dot(lines, gathered[0, :, cut])
            imag = dot(lines, gathered[1, :, cut])
            power = jnp.concatenate([spread[at : at + step, :]] * (lanes // RADIX), 1) * (real * real + imag * imag)
            back = flipped[:, at : at + step]
            parts = [dot(back, (power * real).astype(bf16)), dot(back, (power * imag).astype(bf16))]
            if at == 0:
                total[0, :, cut], total[1, :, cut] = parts
            else:
                total[0, :, cut] += parts[0]
                total[1, :, cut] += parts[1]
    for hop in range(devices):
        rows = pl.ds(pl.multiple_of((me[0, 0] ^ hop) * modes, modes), modes)
        chip, other = divmod(hop, 2)
        target = gives[chip // (chips // 2)].at[chip % (chips // 2)] if other else keeps[chip]
        for c in range(2):
            target[c * modes : (c + 1) * modes, :] = total[c, rows, :].astype(bf16)


def kerr(me, fields, profiles, flipped, weights, modes):
    devices, _, width = fields.shape
    chips = devices // 2
    return pl.pallas_call(
        functools.partial(kerr_kernel, modes, devices, 1024),
        out_shape=[jax.ShapeDtypeStruct((2 * modes, width), bf16)] * chips
        + [jax.ShapeDtypeStruct((chips // 2, 2 * modes, width), bf16)] * 2,
        in_specs=specs("savvv"),
        out_specs=specs("v" * (chips + 2)),
        scratch_shapes=[
            pltpu.VMEM((2, devices * modes, width), bf16),
            pltpu.VMEM((2, devices * modes, width), f32),
            pltpu.VMEM((profiles.shape[0], RADIX), f32),
            pltpu.SemaphoreType.DMA((8 * devices,)),
        ],
        compiler_params=params(),
        name="kerr",
    )(me, fields, profiles, flipped, weights)


def pack_kernel(count, *refs):
    keeps, got, outs = refs[:count], refs[count], refs[count + 1 :]
    skip = got.shape[0] - count
    for at in range(count):
        outs[at][0] = keeps[at][...]
        outs[at][1] = got[skip + at]


def pack(keeps, got):
    count = len(keeps)
    return pl.pallas_call(
        functools.partial(pack_kernel, count),
        out_shape=[jax.ShapeDtypeStruct((2,) + keeps[0].shape, bf16)] * count,
        in_specs=specs("v" * (count + 1)),
        out_specs=specs("v" * count),
        compiler_params=params(),
        name="pack",
    )(*keeps, got)


def first_section(modes, block, source, each, twist, fh, fl, write):
    radix = RADIX
    rows = []
    for slot in range(each):
        at = slice(slot * radix, (slot + 1) * radix)
        rows.append(
            jnp.concatenate([block[c * modes : (c + 1) * modes, at] for c in range(2)], 1)
        )
    block = jnp.concatenate(rows, 0)
    section = dot(block, fh[...]) + dot(block, fl[...])
    for slot in range(each):
        here = slice(slot * modes, (slot + 1) * modes)
        real, imag = section[here, :radix], section[here, radix:]
        row = pl.ds(source * each + slot, 1)
        cosine, sine = twist[0, row, :], twist[1, row, :]
        write(0, slot, real * cosine + imag * sine)
        write(1, slot, imag * cosine - real * sine)


def late_kernel(modes, devices, last, me, factor, base, phase, twist, fh, fl, sh, sl, *rest):
    count = len(groups_of(devices))
    groups, out, (turned, final) = rest[:count], rest[count], rest[count + 1 : count + 3]
    spare = rest[count + 3 :]
    radix = RADIX
    each = radix // devices
    size = each * modes
    length = base.shape[-1]
    for group, hops in zip(groups, groups_of(devices)):
        for at, hop in enumerate(hops):
            source = me[0, 0] ^ hop

            def write(c, slot, values, source=source):
                rows = pl.ds(pl.multiple_of(source * size + slot * modes, modes), modes)
                turned[c, rows, :] = values

            first_section(modes, group.at[at], source, each, twist, fh, fl, write)
    for pair in range(modes // 2):
        both = []
        for m in (2 * pair, 2 * pair + 1):
            both.append(
                jnp.concatenate([turned[c, pl.ds(m, radix, stride=modes), :] for c in range(2)], 0)
            )
        high, low = split(jnp.concatenate(both, 1))
        section = dot(sh[...], high) + (dot(sh[...], low) + dot(sl[...], high))
        for side in range(2):
            for c in range(2):
                final[c, pl.ds(2 * pair + side, radix, stride=modes), :] = section[
                    c * radix : (c + 1) * radix, side * radix : (side + 1) * radix
                ]
    result = spare[0] if last else out

    def finish(k1, carry):
        at = pl.ds(pl.multiple_of(k1 * radix, radix), radix)
        rows = pl.ds(pl.multiple_of(k1 * modes, modes), modes)
        sine, cosine = sincos(phase[:, at] * factor[0, 0])
        real, imag = final[0, rows, :], final[1, rows, :]
        result[0, :, at] = base[0, :, at] + (real * cosine + imag * sine)
        result[1, :, at] = base[1, :, at] + (imag * cosine - real * sine)
        return carry

    copies = []
    for at in range(STRIPES):
        cut = stripe(at, length)
        part = radix // STRIPES
        lax.fori_loop(at * part, (at + 1) * part, finish, 0, unroll=4)
        if last:
            copies.append(
                pltpu.make_async_copy(result.at[:, :, cut], out.at[:, :, cut], spare[1].at[at])
            )
            copies[-1].start()
    for copy in copies:
        copy.wait()


def late(me, factor, groups, base, phase, devices, last):
    _, modes, length = base.shape
    table = tables(length)
    spare = [pltpu.VMEM(base.shape, f32), pltpu.SemaphoreType.DMA((STRIPES,))]
    return pl.pallas_call(
        functools.partial(late_kernel, modes, devices, last),
        out_shape=jax.ShapeDtypeStruct(base.shape, f32),
        in_specs=specs("ssvvvvvvv" + "v" * len(groups)),
        out_specs=specs("h" if last else "v")[0],
        scratch_shapes=[pltpu.VMEM((2, RADIX * modes, RADIX), f32)] * 2 + (spare if last else []),
        compiler_params=params(),
        name="late",
    )(
        me,
        factor,
        base,
        phase,
        table["twist"],
        *table["fwd_first"],
        *table["fwd_second"],
        *groups,
    )


def regular(modes, devices):
    return modes % 16 == 0 and devices & (devices - 1) == 0 and 8 <= devices <= RADIX


def matrix(name, length):
    high, low = tables(length)[name]
    return high.astype(np.float32) + low.astype(np.float32)


def einsum(text, left, right):
    return jnp.einsum(text, left, right, precision=lax.Precision.HIGHEST)


def inverse_plain(factor, launch, phase, devices):
    _, modes, length = launch.shape
    twist = tables(length)["twist"]
    angle = phase * factor[0, 0]
    cosine, sine = jnp.cos(angle), jnp.sin(angle)
    real = launch[0] * cosine - launch[1] * sine
    imag = launch[0] * sine + launch[1] * cosine
    both = jnp.stack([real, imag]).reshape(2, modes, RADIX, -1)
    first = matrix("inv_first", length).reshape(2, RADIX, 2, RADIX)
    real, imag = einsum("dtck,cmkj->dmtj", first, both)
    both = jnp.stack([real * twist[0] - imag * twist[1], real * twist[1] + imag * twist[0]])
    other = length // RADIX
    second = matrix("inv_second", length).reshape(2, other, 2, other)
    both = einsum("cmtj,cjdu->dmtu", both, second).astype(bf16)
    both = both.reshape(2, modes, devices, -1)
    return both.transpose(2, 0, 1, 3).reshape(devices, 2 * modes, -1)


def kerr_plain(fields, profiles, weights, modes):
    devices, _, width = fields.shape
    fields = fields.reshape(devices, 2, modes, width).swapaxes(0, 1)
    fields = fields.reshape(2, devices * modes, width)
    expanded = jnp.einsum("pm,cmt->cpt", profiles, fields, preferred_element_type=f32)
    power = weights * (expanded[0] * expanded[0] + expanded[1] * expanded[1])
    cubed = (power * expanded).astype(bf16)
    projected = jnp.einsum("pm,cpt->cmt", profiles, cubed, preferred_element_type=f32)
    projected = projected.astype(bf16).reshape(2, devices, modes, width)
    return projected.swapaxes(0, 1).reshape(devices, 2 * modes, width)


def forward_plain(factor, base, phase, piece, devices):
    _, modes, length = base.shape
    other = length // RADIX
    twist = tables(length)["twist"]
    both = piece.astype(f32).reshape(devices, 2, modes, -1, other)
    both = both.transpose(1, 2, 0, 3, 4).reshape(2, modes, RADIX, other)
    first = matrix("fwd_first", length).reshape(2, other, 2, other)
    real, imag = einsum("cmtu,cudj->dmtj", both, first)
    both = jnp.stack([real * twist[0] + imag * twist[1], imag * twist[0] - real * twist[1]])
    second = matrix("fwd_second", length).reshape(2, RADIX, 2, RADIX)
    real, imag = einsum("dkct,cmtj->dmkj", second, both).reshape(2, modes, length)
    angle = phase * factor[0, 0]
    cosine, sine = jnp.cos(angle), jnp.sin(angle)
    return base + jnp.stack([real * cosine + imag * sine, imag * cosine - real * sine])


def scalar(value, dtype=f32):
    return value.astype(dtype).reshape(1, 1)


def onward(values, points):
    held = []
    for shift in range(1, points):
        pairs = [(k, k + shift) for k in range(points - shift)]
        held.append(lax.ppermute(values, "gz", pairs))
    return held


def on_device_plain(devices, points, launch, phase, profiles, weights):
    _, modes, _ = launch.shape
    place = lax.axis_index("gz")
    exchange = functools.partial(
        lax.all_to_all, axis_name="modes", split_axis=0, concat_axis=0, tiled=True
    )
    piece = exchange(inverse_plain(scalar(place + 1), launch, phase, devices))
    piece = exchange(kerr_plain(piece, profiles, weights[:, None], modes))
    result = forward_plain(scalar(place + 1), launch, phase, piece, devices)
    for shift, held in enumerate(onward(piece, points), 1):
        result = forward_plain(scalar(place + 1 - shift), result, phase, held, devices)
    return result[None]


def quarters(devices):
    part = devices // 8
    return [tuple(range(at * part, (at + 1) * part)) for at in range(4)]


def chips_of(devices):
    near, close, middle, far = quarters(devices)
    return [near] + [middle] + [close] + [(chip,) for chip in far]


def groups_of(devices):
    return [
        tuple(2 * chip + core for chip in chips for core in range(2))
        for chips in chips_of(devices)
    ]


def on_device(devices, points, launch, phase, profiles, weights):
    _, modes, _ = launch.shape
    if not regular(modes, devices):
        return on_device_plain(devices, points, launch, phase, profiles, weights)
    place = lax.axis_index("gz")
    me = lax.axis_index("modes")
    here = scalar(me, jnp.int32)
    fields = inverse(scalar(place + 1), launch, phase, devices)
    fields = lax.all_to_all(fields, "modes", 0, 0, tiled=True)
    sent = kerr(here, fields, profiles, profiles.T, weights.reshape(-1, RADIX), modes)
    chips = devices // 2
    keeps, (near, far) = sent[:chips], sent[chips:]
    swap = [(a, a ^ 1) for a in range(devices)]
    far = lax.ppermute(far, "modes", swap)
    near = lax.ppermute(near, "modes", swap)
    got = [jnp.stack([keeps[0], near[0]])]
    got += pack(keeps[1 : chips // 2], near) + pack(keeps[chips // 2 :], far)
    for chip in range(1, chips):
        pairs = [(a, a ^ (2 * chip)) for a in range(devices)]
        got[chip] = lax.ppermute(got[chip], "modes", pairs)
    waiting = []
    for group in chips_of(devices):
        pieces = jnp.concatenate([got[chip] for chip in group], 0)
        waiting.append([pieces] + onward(pieces, points))
    result = launch
    for shift in range(points):
        result = late(
            here,
            scalar(place + 1 - shift),
            [held[shift] for held in waiting],
            result,
            phase,
            devices,
            shift == points - 1,
        )
    return result[None]


def solution(mesh):
    in_specs = (P(None, "modes", None), P("modes", None), P(), P())
    out_specs = P("gz", None, "modes", None)
    devices, points = mesh.shape["modes"], mesh.shape["gz"]
    body = functools.partial(on_device, devices, points)
    return jax.shard_map(body, mesh=mesh, in_specs=in_specs, out_specs=out_specs, check_vma=False)
```

```python
import functools
import math

import jax
import jax.numpy as jnp
import numpy as np
from jax import lax
from jax.experimental import pallas as pl
from jax.experimental.pallas import tpu as pltpu
from jax.sharding import PartitionSpec as P

RADIX = 128
STRIPES = 8
HALVES = 4
KSTEP = 256
KTILE = 512
SPACES = pltpu.MemorySpace

f32 = jnp.float32
bf16 = jnp.bfloat16


def halves(table):
    high = table.astype(jnp.bfloat16)
    low = (table - high.astype(np.float64)).astype(jnp.bfloat16)
    return high, low


@functools.lru_cache(None)
def tables(length):
    radix = RADIX
    other = length // radix
    index = np.arange(radix)
    second = np.arange(other)
    scale = 1.0 / math.sqrt(length)
    angle = 2.0 * math.pi / radix * (index[:, None] * index[None, :] % radix)
    cos, sin = np.cos(angle), np.sin(angle)
    last = 2.0 * math.pi / other * (second[:, None] * second[None, :] % other)
    cos2, sin2 = np.cos(last), np.sin(last)
    turn = 2.0 * math.pi / length * (index[:, None] * second[None, :] % length)
    twist = np.stack([np.cos(turn), np.sin(turn)]).astype(np.float32)
    inv_first = np.block([[cos, -sin], [sin, cos]])
    inv_second = np.block([[cos2, sin2], [-sin2, cos2]]) * scale
    fwd_first = np.block([[sin2, cos2], [-cos2, sin2]])
    fwd_second = np.block([[cos, sin], [-sin, cos]]) * scale
    return dict(
        twist=twist,
        inv_first=halves(inv_first),
        inv_second=halves(inv_second),
        fwd_first=halves(fwd_first),
        fwd_second=halves(fwd_second),
    )


def split(values):
    high = values.astype(bf16)
    return high, (values - high.astype(f32)).astype(bf16)


def dot(left, right):
    return lax.dot_general(left, right, (((1,), (0,)), ((), ())), preferred_element_type=f32)


TWO_PI = 2.0 * math.pi
TWO_PI_HIGH = float(np.float32(6.28125))
TWO_PI_LOW = TWO_PI - TWO_PI_HIGH
SIN_TERMS = [(-1) ** n / math.factorial(2 * n + 1) for n in range(6)]
COS_TERMS = [(-1) ** n / math.factorial(2 * n) for n in range(7)]


def sincos(phase):
    turns = jnp.round(phase * (1.0 / TWO_PI))
    rest = (phase - turns * TWO_PI_HIGH) - turns * TWO_PI_LOW
    half = 0.5 * rest
    square = half * half
    sine = SIN_TERMS[-1]
    for term in SIN_TERMS[-2::-1]:
        sine = sine * square + term
    sine = sine * half
    cosine = COS_TERMS[-1]
    for term in COS_TERMS[-2::-1]:
        cosine = cosine * square + term
    twice = sine + sine
    return twice * cosine, 1.0 - twice * sine


def specs(text):
    spaces = dict(s=SPACES.SMEM, v=SPACES.VMEM, h=SPACES.HBM, a=pl.ANY)
    return [pl.BlockSpec(memory_space=spaces[letter]) for letter in text]


def params():
    return pltpu.CompilerParams(vmem_limit_bytes=48 * 1024 * 1024)


def stripe(at, length):
    width = length // STRIPES
    return slice(at * width, (at + 1) * width)


def inverse_kernel(modes, devices, factor, launch, phase, *rest):
    tables_in, out, natural, turned, launched, phases = rest[:5], *rest[5:10]
    tables_here, sems, table_sems = rest[10:15], rest[15], rest[16]
    radix = RADIX
    length = launch.shape[-1]
    half = modes // 2
    copies = []
    for side in range(2):
        rows = slice(side * half, (side + 1) * half)
        for at in range(HALVES):
            width = length // HALVES
            cut = slice(at * width, (at + 1) * width)
            sem = 2 * (side * HALVES + at)
            copies.append(
                [
                    pltpu.make_async_copy(
                        launch.at[:, rows, cut], launched.at[:, rows, cut], sems.at[sem]
                    ),
                    pltpu.make_async_copy(
                        phase.at[rows, cut], phases.at[rows, cut], sems.at[sem + 1]
                    ),
                ]
            )
            for copy in copies[-1]:
                copy.start()
        if side == 0:
            more = [
                pltpu.make_async_copy(there, here, table_sems.at[at])
                for at, (there, here) in enumerate(zip(tables_in, tables_here))
            ]
            for copy in more:
                copy.start()
    twist, fh, fl, sh, sl = tables_here
    for side in range(2):

        def rotate(k1, carry, side=side):
            at = pl.ds(pl.multiple_of(k1 * radix, radix), radix)
            rows = pl.ds(pl.multiple_of(k1 * half, half), half)
            mine = slice(side * half, (side + 1) * half)
            sine, cosine = sincos(phases[mine, at] * factor[0, 0])
            real, imag = launched[0, mine, at], launched[1, mine, at]
            natural[0, rows, :] = real * cosine - imag * sine
            natural[1, rows, :] = real * sine + imag * cosine
            return carry

        for at in range(HALVES):
            for copy in copies[side * HALVES + at]:
                copy.wait()
            part = radix // HALVES
            lax.fori_loop(at * part, (at + 1) * part, rotate, 0, unroll=8)
        if side == 0:
            for copy in more:
                copy.wait()
        for pair in range(half // 2):
            both = []
            for m in (2 * pair, 2 * pair + 1):
                both.append(
                    jnp.concatenate(
                        [natural[c, pl.ds(m, radix, stride=half), :] for c in range(2)], 0
                    )
                )
            high, low = split(jnp.concatenate(both, 1))
            section = dot(fh[...], high) + (dot(fh[...], low) + dot(fl[...], high))
            rows = []
            for one in range(2):
                real = section[:radix, one * radix : (one + 1) * radix]
                imag = section[radix:, one * radix : (one + 1) * radix]
                rows.append(
                    jnp.concatenate(
                        [real * twist[0] - imag * twist[1], real * twist[1] + imag * twist[0]], 1
                    )
                )
            high, low = split(jnp.concatenate(rows, 0))
            final = dot(high, sh[...]) + (dot(low, sh[...]) + dot(high, sl[...]))
            for one in range(2):
                m = side * half + 2 * pair + one
                for c in range(2):
                    turned[c, pl.ds(m, radix, stride=modes), :] = final[
                        one * radix : (one + 1) * radix, c * radix : (c + 1) * radix
                    ]
    each = radix // devices
    for t2 in range(radix):
        target, slot = divmod(t2, each)
        for c in range(2):
            out[target, c * modes : (c + 1) * modes, slot * radix : (slot + 1) * radix] = turned[
                c, t2 * modes : (t2 + 1) * modes, :
            ].astype(bf16)


def inverse(factor, launch, phase, devices):
    _, modes, length = launch.shape
    table = tables(length)
    held = [table["twist"], *table["inv_first"], *table["inv_second"]]
    return pl.pallas_call(
        functools.partial(inverse_kernel, modes, devices),
        out_shape=jax.ShapeDtypeStruct((devices, 2 * modes, length // devices), bf16),
        in_specs=specs("shhhhhhh"),
        out_specs=specs("v")[0],
        scratch_shapes=[
            pltpu.VMEM((2, RADIX * modes // 2, RADIX), f32),
            pltpu.VMEM((2, RADIX * modes, RADIX), f32),
            pltpu.VMEM(launch.shape, f32),
            pltpu.VMEM(phase.shape, f32),
            *[pltpu.VMEM(value.shape, value.dtype) for value in held],
            pltpu.SemaphoreType.DMA((4 * HALVES,)),
            pltpu.SemaphoreType.DMA((len(held),)),
        ],
        compiler_params=params(),
        name="inverse",
    )(
        factor,
        *[
            pltpu.with_memory_space_constraint(value, SPACES.HBM)
            for value in (launch, phase, *map(jnp.asarray, held))
        ],
    )


def kerr_kernel(modes, devices, step, lanes, me, fields, profiles, flipped, weights, *rest):
    chips = devices // 2
    keeps, gives = rest[:chips], rest[chips : chips + 2]
    gathered, fields_t, total_t, total, sems = rest[chips + 2 :]
    points, _ = profiles.shape
    width = fields.shape[-1]
    tiles = width // lanes
    copies = []
    for tile in range(tiles):
        cut = slice(tile * lanes, (tile + 1) * lanes)
        for source in range(devices):
            for c in range(2):
                copies.append(
                    pltpu.make_async_copy(
                        fields.at[source, c * modes : (c + 1) * modes, cut],
                        gathered.at[c, source * modes : (source + 1) * modes, cut],
                        sems.at[len(copies)],
                    )
                )
                copies[-1].start()
    for tile in range(tiles):
        cut = slice(tile * lanes, (tile + 1) * lanes)
        for copy in copies[tile * 2 * devices : (tile + 1) * 2 * devices]:
            copy.wait()
        for c in range(2):
            fields_t[c, cut, :] = gathered[c, :, cut].T
    for at in range(0, points, step):
        these = slice(at, at + step)
        for tile in range(tiles):
            cut = slice(tile * lanes, (tile + 1) * lanes)
            real = dot(fields_t[0, cut, :], flipped[:, these])
            imag = dot(fields_t[1, cut, :], flipped[:, these])
            power = weights[:, these] * (real * real + imag * imag)
            parts = [
                dot((power * real).astype(bf16), profiles[these, :]),
                dot((power * imag).astype(bf16), profiles[these, :]),
            ]
            if at == 0:
                total_t[0, cut, :], total_t[1, cut, :] = parts
            else:
                total_t[0, cut, :] += parts[0]
                total_t[1, cut, :] += parts[1]
    for c in range(2):
        for tile in range(width // RADIX):
            cut = slice(tile * RADIX, (tile + 1) * RADIX)
            total[c, :, cut] = total_t[c, cut, :].T
    for hop in range(devices):
        rows = pl.ds(pl.multiple_of((me[0, 0] ^ hop) * modes, modes), modes)
        chip, other = divmod(hop, 2)
        target = gives[chip // (chips // 2)].at[chip % (chips // 2)] if other else keeps[chip]
        for c in range(2):
            target[c * modes : (c + 1) * modes, :] = total[c, rows, :].astype(bf16)


def kerr(me, fields, profiles, flipped, weights, modes):
    devices, _, width = fields.shape
    chips = devices // 2
    return pl.pallas_call(
        functools.partial(kerr_kernel, modes, devices, KSTEP, KTILE),
        out_shape=[jax.ShapeDtypeStruct((2 * modes, width), bf16)] * chips
        + [jax.ShapeDtypeStruct((chips // 2, 2 * modes, width), bf16)] * 2,
        in_specs=specs("savvv"),
        out_specs=specs("v" * (chips + 2)),
        scratch_shapes=[
            pltpu.VMEM((2, devices * modes, width), bf16),
            pltpu.VMEM((2, width, devices * modes), bf16),
            pltpu.VMEM((2, width, devices * modes), f32),
            pltpu.VMEM((2, devices * modes, width), f32),
            pltpu.SemaphoreType.DMA((2 * devices * (width // KTILE),)),
        ],
        compiler_params=params(),
        name="kerr",
    )(me, fields, profiles, flipped, weights)


def pack_kernel(count, *refs):
    keeps, got, outs = refs[:count], refs[count], refs[count + 1 :]
    skip = got.shape[0] - count
    for at in range(count):
        outs[at][0] = keeps[at][...]
        outs[at][1] = got[skip + at]


def pack(keeps, got):
    count = len(keeps)
    return pl.pallas_call(
        functools.partial(pack_kernel, count),
        out_shape=[jax.ShapeDtypeStruct((2,) + keeps[0].shape, bf16)] * count,
        in_specs=specs("v" * (count + 1)),
        out_specs=specs("v" * count),
        compiler_params=params(),
        name="pack",
    )(*keeps, got)


def first_section(modes, block, source, each, twist, fh, fl, write):
    radix = RADIX
    rows = []
    for slot in range(each):
        at = slice(slot * radix, (slot + 1) * radix)
        rows.append(
            jnp.concatenate([block[c * modes : (c + 1) * modes, at] for c in range(2)], 1)
        )
    block = jnp.concatenate(rows, 0)
    section = dot(block, fh[...]) + dot(block, fl[...])
    for slot in range(each):
        here = slice(slot * modes, (slot + 1) * modes)
        real, imag = section[here, :radix], section[here, radix:]
        row = pl.ds(source * each + slot, 1)
        cosine, sine = twist[0, row, :], twist[1, row, :]
        write(0, slot, real * cosine + imag * sine)
        write(1, slot, imag * cosine - real * sine)


def late_kernel(modes, devices, first, alone, last, me, factor, base, phase, *rest):
    (twist, fh, fl, sh, sl), rest = rest[:5], rest[5:]
    count = len(groups_of(devices))
    groups, out, rest = rest[:count], rest[count], rest[count + 1 :]
    if not alone:
        ahead, rest = rest[0], rest[1:]
    turned, final = rest[:2]
    spare = rest[2:]
    radix = RADIX
    each = radix // devices
    size = each * modes
    length = base.shape[-1]
    for group, hops in zip(groups, groups_of(devices)):
        for at, hop in enumerate(hops):
            source = me[0, 0] ^ hop

            def write(c, slot, values, source=source):
                rows = pl.ds(pl.multiple_of(source * size + slot * modes, modes), modes)
                turned[c, rows, :] = values

            first_section(modes, group.at[at], source, each, twist, fh, fl, write)
    for pair in range(modes // 2):
        both = []
        for m in (2 * pair, 2 * pair + 1):
            both.append(
                jnp.concatenate([turned[c, pl.ds(m, radix, stride=modes), :] for c in range(2)], 0)
            )
        high, low = split(jnp.concatenate(both, 1))
        section = dot(sh[...], high) + (dot(sh[...], low) + dot(sl[...], high))
        for side in range(2):
            for c in range(2):
                final[c, pl.ds(2 * pair + side, radix, stride=modes), :] = section[
                    c * radix : (c + 1) * radix, side * radix : (side + 1) * radix
                ]
    result = spare[0] if last else out

    def finish(k1, carry):
        at = pl.ds(pl.multiple_of(k1 * radix, radix), radix)
        rows = pl.ds(pl.multiple_of(k1 * modes, modes), modes)
        if first:
            sine, cosine = sincos(phase[:, at] * factor[0, 0])
        else:
            sine, cosine = phase[0, :, at], phase[1, :, at]
        if not alone:
            ahead[0, :, at], ahead[1, :, at] = sincos(phase[:, at] * (factor[0, 0] - 1.0))
        real, imag = final[0, rows, :], final[1, rows, :]
        result[0, :, at] = base[0, :, at] + (real * cosine + imag * sine)
        result[1, :, at] = base[1, :, at] + (imag * cosine - real * sine)
        return carry

    copies = []
    for at in range(STRIPES):
        cut = stripe(at, length)
        part = radix // STRIPES
        lax.fori_loop(at * part, (at + 1) * part, finish, 0, unroll=4)
        if last:
            copies.append(
                pltpu.make_async_copy(result.at[:, :, cut], out.at[:, :, cut], spare[1].at[at])
            )
            copies[-1].start()
    for copy in copies:
        copy.wait()


def late(me, factor, groups, base, phase, devices, first, last):
    _, modes, length = base.shape
    ahead = first and not last
    table = tables(length)
    spare = [pltpu.VMEM(base.shape, f32), pltpu.SemaphoreType.DMA((STRIPES,))]
    return pl.pallas_call(
        functools.partial(late_kernel, modes, devices, first, not ahead, last),
        out_shape=[jax.ShapeDtypeStruct(base.shape, f32)] * (2 if ahead else 1),
        in_specs=specs("ssvvvvvvv" + "v" * len(groups)),
        out_specs=specs("vv" if ahead else "h" if last else "v"),
        scratch_shapes=[pltpu.VMEM((2, RADIX * modes, RADIX), f32)] * 2 + (spare if last else []),
        compiler_params=params(),
        name="late",
    )(
        me,
        factor,
        base,
        phase,
        table["twist"],
        *table["fwd_first"],
        *table["fwd_second"],
        *groups,
    )


def regular(modes, devices):
    return modes % 16 == 0 and devices & (devices - 1) == 0 and 8 <= devices <= RADIX


def matrix(name, length):
    high, low = tables(length)[name]
    return high.astype(np.float32) + low.astype(np.float32)


def einsum(text, left, right):
    return jnp.einsum(text, left, right, precision=lax.Precision.HIGHEST)


def inverse_plain(factor, launch, phase, devices):
    _, modes, length = launch.shape
    twist = tables(length)["twist"]
    angle = phase * factor[0, 0]
    cosine, sine = jnp.cos(angle), jnp.sin(angle)
    real = launch[0] * cosine - launch[1] * sine
    imag = launch[0] * sine + launch[1] * cosine
    both = jnp.stack([real, imag]).reshape(2, modes, RADIX, -1)
    first = matrix("inv_first", length).reshape(2, RADIX, 2, RADIX)
    real, imag = einsum("dtck,cmkj->dmtj", first, both)
    both = jnp.stack([real * twist[0] - imag * twist[1], real * twist[1] + imag * twist[0]])
    other = length // RADIX
    second = matrix("inv_second", length).reshape(2, other, 2, other)
    both = einsum("cmtj,cjdu->dmtu", both, second).astype(bf16)
    both = both.reshape(2, modes, devices, -1)
    return both.transpose(2, 0, 1, 3).reshape(devices, 2 * modes, -1)


def kerr_plain(fields, profiles, weights, modes):
    devices, _, width = fields.shape
    fields = fields.reshape(devices, 2, modes, width).swapaxes(0, 1)
    fields = fields.reshape(2, devices * modes, width)
    expanded = jnp.einsum("pm,cmt->cpt", profiles, fields, preferred_element_type=f32)
    power = weights * (expanded[0] * expanded[0] + expanded[1] * expanded[1])
    cubed = (power * expanded).astype(bf16)
    projected = jnp.einsum("pm,cpt->cmt", profiles, cubed, preferred_element_type=f32)
    projected = projected.astype(bf16).reshape(2, devices, modes, width)
    return projected.swapaxes(0, 1).reshape(devices, 2 * modes, width)


def forward_plain(factor, base, phase, piece, devices):
    _, modes, length = base.shape
    other = length // RADIX
    twist = tables(length)["twist"]
    both = piece.astype(f32).reshape(devices, 2, modes, -1, other)
    both = both.transpose(1, 2, 0, 3, 4).reshape(2, modes, RADIX, other)
    first = matrix("fwd_first", length).reshape(2, other, 2, other)
    real, imag = einsum("cmtu,cudj->dmtj", both, first)
    both = jnp.stack([real * twist[0] + imag * twist[1], imag * twist[0] - real * twist[1]])
    second = matrix("fwd_second", length).reshape(2, RADIX, 2, RADIX)
    real, imag = einsum("dkct,cmtj->dmkj", second, both).reshape(2, modes, length)
    angle = phase * factor[0, 0]
    cosine, sine = jnp.cos(angle), jnp.sin(angle)
    return base + jnp.stack([real * cosine + imag * sine, imag * cosine - real * sine])


def scalar(value, dtype=f32):
    return value.astype(dtype).reshape(1, 1)


def onward(values, points):
    held = []
    for shift in range(1, points):
        pairs = [(k, k + shift) for k in range(points - shift)]
        held.append(lax.ppermute(values, "gz", pairs))
    return held


def on_device_plain(devices, points, launch, phase, profiles, weights):
    _, modes, _ = launch.shape
    place = lax.axis_index("gz")
    exchange = functools.partial(
        lax.all_to_all, axis_name="modes", split_axis=0, concat_axis=0, tiled=True
    )
    piece = exchange(inverse_plain(scalar(place + 1), launch, phase, devices))
    piece = exchange(kerr_plain(piece, profiles, weights[:, None], modes))
    result = forward_plain(scalar(place + 1), launch, phase, piece, devices)
    for shift, held in enumerate(onward(piece, points), 1):
        result = forward_plain(scalar(place + 1 - shift), result, phase, held, devices)
    return result[None]


def quarters(devices):
    part = devices // 8
    return [tuple(range(at * part, (at + 1) * part)) for at in range(4)]


def chips_of(devices):
    near, close, middle, far = quarters(devices)
    return [near] + [middle] + [close] + [(chip,) for chip in far]


def groups_of(devices):
    return [
        tuple(2 * chip + core for chip in chips for core in range(2))
        for chips in chips_of(devices)
    ]


def on_device(devices, points, launch, phase, profiles, weights):
    _, modes, _ = launch.shape
    if not regular(modes, devices):
        return on_device_plain(devices, points, launch, phase, profiles, weights)
    place = lax.axis_index("gz")
    me = lax.axis_index("modes")
    here = scalar(me, jnp.int32)
    fields = inverse(scalar(place + 1), launch, phase, devices)
    fields = lax.all_to_all(fields, "modes", 0, 0, tiled=True)
    sent = kerr(here, fields, profiles, profiles.T, weights[None, :], modes)
    chips = devices // 2
    keeps, (near, far) = sent[:chips], sent[chips:]
    swap = [(a, a ^ 1) for a in range(devices)]
    far = lax.ppermute(far, "modes", swap)
    near = lax.ppermute(near, "modes", swap)
    got = [jnp.stack([keeps[0], near[0]])]
    got += pack(keeps[1 : chips // 2], near) + pack(keeps[chips // 2 :], far)
    for chip in range(1, chips):
        pairs = [(a, a ^ (2 * chip)) for a in range(devices)]
        got[chip] = lax.ppermute(got[chip], "modes", pairs)
    waiting = []
    for group in chips_of(devices):
        pieces = jnp.concatenate([got[chip] for chip in group], 0)
        waiting.append([pieces] + onward(pieces, points))
    result = launch
    for shift in range(points):
        last = shift == points - 1
        result, *ahead = late(
            here,
            scalar(place + 1 - shift),
            [held[shift] for held in waiting],
            result,
            turn if shift == 1 else phase,
            devices,
            shift != 1,
            last,
        )
        if ahead:
            turn = ahead[0]
    return result[None]


def solution(mesh):
    in_specs = (P(None, "modes", None), P("modes", None), P(), P())
    out_specs = P("gz", None, "modes", None)
    devices, points = mesh.shape["modes"], mesh.shape["gz"]
    body = functools.partial(on_device, devices, points)
    return jax.shard_map(body, mesh=mesh, in_specs=in_specs, out_specs=out_specs, check_vma=False)
```

```python
import functools
import math

import jax
import jax.numpy as jnp
import numpy as np
from jax import lax
from jax.experimental import pallas as pl
from jax.experimental.pallas import tpu as pltpu
from jax.sharding import PartitionSpec as P

RADIX = 128
STRIPES = 8
HALVES = 4
KSTEP = 256
KTILE = 512
SPACES = pltpu.MemorySpace

f32 = jnp.float32
bf16 = jnp.bfloat16


def halves(table):
    high = table.astype(jnp.bfloat16)
    low = (table - high.astype(np.float64)).astype(jnp.bfloat16)
    return high, low


@functools.lru_cache(None)
def tables(length):
    radix = RADIX
    other = length // radix
    index = np.arange(radix)
    second = np.arange(other)
    scale = 1.0 / math.sqrt(length)
    angle = 2.0 * math.pi / radix * (index[:, None] * index[None, :] % radix)
    cos, sin = np.cos(angle), np.sin(angle)
    last = 2.0 * math.pi / other * (second[:, None] * second[None, :] % other)
    cos2, sin2 = np.cos(last), np.sin(last)
    turn = 2.0 * math.pi / length * (index[:, None] * second[None, :] % length)
    twist = np.stack([np.cos(turn), np.sin(turn)]).astype(np.float32)
    inv_first = np.block([[cos, -sin], [sin, cos]])
    inv_second = np.block([[cos2, sin2], [-sin2, cos2]]) * scale
    fwd_first = np.block([[sin2, cos2], [-cos2, sin2]])
    fwd_second = np.block([[cos, sin], [-sin, cos]]) * scale
    return dict(
        twist=twist,
        inv_first=halves(inv_first),
        inv_second=halves(inv_second),
        fwd_first=halves(fwd_first),
        fwd_second=halves(fwd_second),
    )


def split(values):
    high = values.astype(bf16)
    return high, (values - high.astype(f32)).astype(bf16)


def dot(left, right):
    return lax.dot_general(left, right, (((1,), (0,)), ((), ())), preferred_element_type=f32)


TWO_PI = 2.0 * math.pi
TWO_PI_HIGH = float(np.float32(6.28125))
TWO_PI_LOW = TWO_PI - TWO_PI_HIGH
SIN_TERMS = [(-1) ** n / math.factorial(2 * n + 1) for n in range(6)]
COS_TERMS = [(-1) ** n / math.factorial(2 * n) for n in range(7)]


def sincos(phase):
    turns = jnp.round(phase * (1.0 / TWO_PI))
    rest = (phase - turns * TWO_PI_HIGH) - turns * TWO_PI_LOW
    half = 0.5 * rest
    square = half * half
    sine = SIN_TERMS[-1]
    for term in SIN_TERMS[-2::-1]:
        sine = sine * square + term
    sine = sine * half
    cosine = COS_TERMS[-1]
    for term in COS_TERMS[-2::-1]:
        cosine = cosine * square + term
    twice = sine + sine
    return twice * cosine, 1.0 - twice * sine


def specs(text):
    spaces = dict(s=SPACES.SMEM, v=SPACES.VMEM, h=SPACES.HBM, a=pl.ANY)
    return [pl.BlockSpec(memory_space=spaces[letter]) for letter in text]


def params():
    return pltpu.CompilerParams(vmem_limit_bytes=48 * 1024 * 1024)


def stripe(at, length):
    width = length // STRIPES
    return slice(at * width, (at + 1) * width)


def inverse_kernel(modes, devices, factor, launch, phase, *rest):
    tables_in, out, natural, turned, launched, phases = rest[:5], *rest[5:10]
    tables_here, sems, table_sems = rest[10:15], rest[15], rest[16]
    radix = RADIX
    length = launch.shape[-1]
    half = modes // 2
    copies = []
    for side in range(2):
        rows = slice(side * half, (side + 1) * half)
        for at in range(HALVES):
            width = length // HALVES
            cut = slice(at * width, (at + 1) * width)
            sem = 2 * (side * HALVES + at)
            copies.append(
                [
                    pltpu.make_async_copy(
                        launch.at[:, rows, cut], launched.at[:, rows, cut], sems.at[sem]
                    ),
                    pltpu.make_async_copy(
                        phase.at[rows, cut], phases.at[rows, cut], sems.at[sem + 1]
                    ),
                ]
            )
            for copy in copies[-1]:
                copy.start()
        if side == 0:
            more = [
                pltpu.make_async_copy(there, here, table_sems.at[at])
                for at, (there, here) in enumerate(zip(tables_in, tables_here))
            ]
            for copy in more:
                copy.start()
    twist, fh, fl, sh, sl = tables_here
    for side in range(2):

        def rotate(k1, carry, side=side):
            at = pl.ds(pl.multiple_of(k1 * radix, radix), radix)
            rows = pl.ds(pl.multiple_of(k1 * half, half), half)
            mine = slice(side * half, (side + 1) * half)
            sine, cosine = sincos(phases[mine, at] * factor[0, 0])
            real, imag = launched[0, mine, at], launched[1, mine, at]
            natural[0, rows, :] = real * cosine - imag * sine
            natural[1, rows, :] = real * sine + imag * cosine
            return carry

        for at in range(HALVES):
            for copy in copies[side * HALVES + at]:
                copy.wait()
            part = radix // HALVES
            lax.fori_loop(at * part, (at + 1) * part, rotate, 0, unroll=8)
        if side == 0:
            for copy in more:
                copy.wait()
        for pair in range(half // 2):
            both = []
            for m in (2 * pair, 2 * pair + 1):
                both.append(
                    jnp.concatenate(
                        [natural[c, pl.ds(m, radix, stride=half), :] for c in range(2)], 0
                    )
                )
            high, low = split(jnp.concatenate(both, 1))
            section = dot(fh[...], high) + (dot(fh[...], low) + dot(fl[...], high))
            rows = []
            for one in range(2):
                real = section[:radix, one * radix : (one + 1) * radix]
                imag = section[radix:, one * radix : (one + 1) * radix]
                rows.append(
                    jnp.concatenate(
                        [real * twist[0] - imag * twist[1], real * twist[1] + imag * twist[0]], 1
                    )
                )
            high, low = split(jnp.concatenate(rows, 0))
            final = dot(high, sh[...]) + (dot(low, sh[...]) + dot(high, sl[...]))
            for one in range(2):
                m = side * half + 2 * pair + one
                for c in range(2):
                    turned[c, pl.ds(m, radix, stride=modes), :] = final[
                        one * radix : (one + 1) * radix, c * radix : (c + 1) * radix
                    ]
    each = radix // devices
    for t2 in range(radix):
        target, slot = divmod(t2, each)
        for c in range(2):
            out[target, c * modes : (c + 1) * modes, slot * radix : (slot + 1) * radix] = turned[
                c, t2 * modes : (t2 + 1) * modes, :
            ].astype(bf16)


def inverse(factor, launch, phase, devices):
    _, modes, length = launch.shape
    table = tables(length)
    held = [table["twist"], *table["inv_first"], *table["inv_second"]]
    return pl.pallas_call(
        functools.partial(inverse_kernel, modes, devices),
        out_shape=jax.ShapeDtypeStruct((devices, 2 * modes, length // devices), bf16),
        in_specs=specs("shhhhhhh"),
        out_specs=specs("v")[0],
        scratch_shapes=[
            pltpu.VMEM((2, RADIX * modes // 2, RADIX), f32),
            pltpu.VMEM((2, RADIX * modes, RADIX), f32),
            pltpu.VMEM(launch.shape, f32),
            pltpu.VMEM(phase.shape, f32),
            *[pltpu.VMEM(value.shape, value.dtype) for value in held],
            pltpu.SemaphoreType.DMA((4 * HALVES,)),
            pltpu.SemaphoreType.DMA((len(held),)),
        ],
        compiler_params=params(),
        name="inverse",
    )(
        factor,
        *[
            pltpu.with_memory_space_constraint(value, SPACES.HBM)
            for value in (launch, phase, *map(jnp.asarray, held))
        ],
    )


def kerr_kernel(modes, devices, step, lanes, me, fields, profiles, flipped, weights, *rest):
    chips = devices // 2
    keeps, gives = rest[:chips], rest[chips : chips + 2]
    gathered, fields_t, total_t, total, sems = rest[chips + 2 :]
    points, _ = profiles.shape
    width = fields.shape[-1]
    tiles = width // lanes
    copies = []
    for tile in range(tiles):
        cut = slice(tile * lanes, (tile + 1) * lanes)
        for source in range(devices):
            for c in range(2):
                copies.append(
                    pltpu.make_async_copy(
                        fields.at[source, c * modes : (c + 1) * modes, cut],
                        gathered.at[c, source * modes : (source + 1) * modes, cut],
                        sems.at[len(copies)],
                    )
                )
                copies[-1].start()
    for tile in range(tiles):
        cut = slice(tile * lanes, (tile + 1) * lanes)
        for copy in copies[tile * 2 * devices : (tile + 1) * 2 * devices]:
            copy.wait()
        for c in range(2):
            fields_t[c, cut, :] = gathered[c, :, cut].T
    for at in range(0, points, step):
        these = slice(at, at + step)
        for tile in range(tiles):
            cut = slice(tile * lanes, (tile + 1) * lanes)
            real = dot(fields_t[0, cut, :], flipped[:, these])
            imag = dot(fields_t[1, cut, :], flipped[:, these])
            power = weights[:, these] * (real * real + imag * imag)
            parts = [
                dot((power * real).astype(bf16), profiles[these, :]),
                dot((power * imag).astype(bf16), profiles[these, :]),
            ]
            if at == 0:
                total_t[0, cut, :], total_t[1, cut, :] = parts
            else:
                total_t[0, cut, :] += parts[0]
                total_t[1, cut, :] += parts[1]
    for c in range(2):
        for tile in range(width // RADIX):
            cut = slice(tile * RADIX, (tile + 1) * RADIX)
            total[c, :, cut] = total_t[c, cut, :].T
    for hop in range(devices):
        rows = pl.ds(pl.multiple_of((me[0, 0] ^ hop) * modes, modes), modes)
        chip, other = divmod(hop, 2)
        target = gives[chip // (chips // 2)].at[chip % (chips // 2)] if other else keeps[chip]
        for c in range(2):
            target[c * modes : (c + 1) * modes, :] = total[c, rows, :].astype(bf16)


def kerr(me, fields, profiles, flipped, weights, modes):
    devices, _, width = fields.shape
    chips = devices // 2
    return pl.pallas_call(
        functools.partial(kerr_kernel, modes, devices, KSTEP, KTILE),
        out_shape=[jax.ShapeDtypeStruct((2 * modes, width), bf16)] * chips
        + [jax.ShapeDtypeStruct((chips // 2, 2 * modes, width), bf16)] * 2,
        in_specs=specs("savvv"),
        out_specs=specs("v" * (chips + 2)),
        scratch_shapes=[
            pltpu.VMEM((2, devices * modes, width), bf16),
            pltpu.VMEM((2, width, devices * modes), bf16),
            pltpu.VMEM((2, width, devices * modes), f32),
            pltpu.VMEM((2, devices * modes, width), f32),
            pltpu.SemaphoreType.DMA((2 * devices * (width // KTILE),)),
        ],
        compiler_params=params(),
        name="kerr",
    )(me, fields, profiles, flipped, weights)


def pack_kernel(count, *refs):
    keeps, got, outs = refs[:count], refs[count], refs[count + 1 :]
    skip = got.shape[0] - count
    for at in range(count):
        outs[at][0] = keeps[at][...]
        outs[at][1] = got[skip + at]


def pack(keeps, got):
    count = len(keeps)
    return pl.pallas_call(
        functools.partial(pack_kernel, count),
        out_shape=[jax.ShapeDtypeStruct((2,) + keeps[0].shape, bf16)] * count,
        in_specs=specs("v" * (count + 1)),
        out_specs=specs("v" * count),
        compiler_params=params(),
        name="pack",
    )(*keeps, got)


def first_section(modes, block, source, each, twist, fh, fl, write):
    radix = RADIX
    rows = []
    for slot in range(each):
        at = slice(slot * radix, (slot + 1) * radix)
        rows.append(
            jnp.concatenate([block[c * modes : (c + 1) * modes, at] for c in range(2)], 1)
        )
    block = jnp.concatenate(rows, 0)
    section = dot(block, fh[...]) + dot(block, fl[...])
    for slot in range(each):
        here = slice(slot * modes, (slot + 1) * modes)
        real, imag = section[here, :radix], section[here, radix:]
        row = pl.ds(source * each + slot, 1)
        cosine, sine = twist[0, row, :], twist[1, row, :]
        write(0, slot, real * cosine + imag * sine)
        write(1, slot, imag * cosine - real * sine)


def late_kernel(modes, devices, first, alone, last, me, factor, base, phase, *rest):
    (twist, fh, fl, sh, sl), rest = rest[:5], rest[5:]
    count = len(groups_of(devices))
    groups, out, rest = rest[:count], rest[count], rest[count + 1 :]
    if not alone:
        ahead, rest = rest[0], rest[1:]
    turned, final = rest[:2]
    spare = rest[2:]
    length = base.shape[-1]
    inward = []
    if not first:
        *spare, turns, arrive = spare
        for at in range(STRIPES):
            cut = stripe(at, length)
            inward.append(
                pltpu.make_async_copy(phase.at[:, :, cut], turns.at[:, :, cut], arrive.at[at])
            )
            inward[-1].start()
    radix = RADIX
    each = radix // devices
    size = each * modes
    length = base.shape[-1]
    for group, hops in zip(groups, groups_of(devices)):
        for at, hop in enumerate(hops):
            source = me[0, 0] ^ hop

            def write(c, slot, values, source=source):
                rows = pl.ds(pl.multiple_of(source * size + slot * modes, modes), modes)
                turned[c, rows, :] = values

            first_section(modes, group.at[at], source, each, twist, fh, fl, write)
    for pair in range(modes // 2):
        both = []
        for m in (2 * pair, 2 * pair + 1):
            both.append(
                jnp.concatenate([turned[c, pl.ds(m, radix, stride=modes), :] for c in range(2)], 0)
            )
        high, low = split(jnp.concatenate(both, 1))
        section = dot(sh[...], high) + (dot(sh[...], low) + dot(sl[...], high))
        for side in range(2):
            for c in range(2):
                final[c, pl.ds(2 * pair + side, radix, stride=modes), :] = section[
                    c * radix : (c + 1) * radix, side * radix : (side + 1) * radix
                ]
    result = spare[0] if last else out

    def finish(k1, carry):
        at = pl.ds(pl.multiple_of(k1 * radix, radix), radix)
        rows = pl.ds(pl.multiple_of(k1 * modes, modes), modes)
        if first:
            sine, cosine = sincos(phase[:, at] * factor[0, 0])
        else:
            sine, cosine = turns[0, :, at], turns[1, :, at]
        if not alone:
            ahead[0, :, at], ahead[1, :, at] = sincos(phase[:, at] * (factor[0, 0] - 1.0))
        real, imag = final[0, rows, :], final[1, rows, :]
        result[0, :, at] = base[0, :, at] + (real * cosine + imag * sine)
        result[1, :, at] = base[1, :, at] + (imag * cosine - real * sine)
        return carry

    copies = []
    for at in range(STRIPES):
        cut = stripe(at, length)
        part = radix // STRIPES
        if not first:
            inward[at].wait()
        lax.fori_loop(at * part, (at + 1) * part, finish, 0, unroll=4)
        if last:
            copies.append(
                pltpu.make_async_copy(result.at[:, :, cut], out.at[:, :, cut], spare[1].at[at])
            )
            copies[-1].start()
    for copy in copies:
        copy.wait()


def late(me, factor, groups, base, phase, devices, first, last):
    _, modes, length = base.shape
    ahead = first and not last
    table = tables(length)
    spare = [pltpu.VMEM(base.shape, f32), pltpu.SemaphoreType.DMA((STRIPES,))]
    spare = spare * last + spare * (not first)
    if not first:
        phase = pltpu.with_memory_space_constraint(phase, SPACES.HBM)
    return pl.pallas_call(
        functools.partial(late_kernel, modes, devices, first, not ahead, last),
        out_shape=[jax.ShapeDtypeStruct(base.shape, f32)] * (2 if ahead else 1),
        in_specs=specs("ssv" + ("v" if first else "h") + "vvvvv" + "v" * len(groups)),
        out_specs=specs("vv" if ahead else "h" if last else "v"),
        scratch_shapes=[pltpu.VMEM((2, RADIX * modes, RADIX), f32)] * 2 + spare,
        compiler_params=params(),
        name="late",
    )(
        me,
        factor,
        base,
        phase,
        table["twist"],
        *table["fwd_first"],
        *table["fwd_second"],
        *groups,
    )


def regular(modes, devices):
    return modes % 16 == 0 and devices & (devices - 1) == 0 and 8 <= devices <= RADIX


def matrix(name, length):
    high, low = tables(length)[name]
    return high.astype(np.float32) + low.astype(np.float32)


def einsum(text, left, right):
    return jnp.einsum(text, left, right, precision=lax.Precision.HIGHEST)


def inverse_plain(factor, launch, phase, devices):
    _, modes, length = launch.shape
    twist = tables(length)["twist"]
    angle = phase * factor[0, 0]
    cosine, sine = jnp.cos(angle), jnp.sin(angle)
    real = launch[0] * cosine - launch[1] * sine
    imag = launch[0] * sine + launch[1] * cosine
    both = jnp.stack([real, imag]).reshape(2, modes, RADIX, -1)
    first = matrix("inv_first", length).reshape(2, RADIX, 2, RADIX)
    real, imag = einsum("dtck,cmkj->dmtj", first, both)
    both = jnp.stack([real * twist[0] - imag * twist[1], real * twist[1] + imag * twist[0]])
    other = length // RADIX
    second = matrix("inv_second", length).reshape(2, other, 2, other)
    both = einsum("cmtj,cjdu->dmtu", both, second).astype(bf16)
    both = both.reshape(2, modes, devices, -1)
    return both.transpose(2, 0, 1, 3).reshape(devices, 2 * modes, -1)


def kerr_plain(fields, profiles, weights, modes):
    devices, _, width = fields.shape
    fields = fields.reshape(devices, 2, modes, width).swapaxes(0, 1)
    fields = fields.reshape(2, devices * modes, width)
    expanded = jnp.einsum("pm,cmt->cpt", profiles, fields, preferred_element_type=f32)
    power = weights * (expanded[0] * expanded[0] + expanded[1] * expanded[1])
    cubed = (power * expanded).astype(bf16)
    projected = jnp.einsum("pm,cpt->cmt", profiles, cubed, preferred_element_type=f32)
    projected = projected.astype(bf16).reshape(2, devices, modes, width)
    return projected.swapaxes(0, 1).reshape(devices, 2 * modes, width)


def forward_plain(factor, base, phase, piece, devices):
    _, modes, length = base.shape
    other = length // RADIX
    twist = tables(length)["twist"]
    both = piece.astype(f32).reshape(devices, 2, modes, -1, other)
    both = both.transpose(1, 2, 0, 3, 4).reshape(2, modes, RADIX, other)
    first = matrix("fwd_first", length).reshape(2, other, 2, other)
    real, imag = einsum("cmtu,cudj->dmtj", both, first)
    both = jnp.stack([real * twist[0] + imag * twist[1], imag * twist[0] - real * twist[1]])
    second = matrix("fwd_second", length).reshape(2, RADIX, 2, RADIX)
    real, imag = einsum("dkct,cmtj->dmkj", second, both).reshape(2, modes, length)
    angle = phase * factor[0, 0]
    cosine, sine = jnp.cos(angle), jnp.sin(angle)
    return base + jnp.stack([real * cosine + imag * sine, imag * cosine - real * sine])


def scalar(value, dtype=f32):
    return value.astype(dtype).reshape(1, 1)


def onward(values, points):
    held = []
    for shift in range(1, points):
        pairs = [(k, k + shift) for k in range(points - shift)]
        held.append(lax.ppermute(values, "gz", pairs))
    return held


def on_device_plain(devices, points, launch, phase, profiles, weights):
    _, modes, _ = launch.shape
    place = lax.axis_index("gz")
    exchange = functools.partial(
        lax.all_to_all, axis_name="modes", split_axis=0, concat_axis=0, tiled=True
    )
    piece = exchange(inverse_plain(scalar(place + 1), launch, phase, devices))
    piece = exchange(kerr_plain(piece, profiles, weights[:, None], modes))
    result = forward_plain(scalar(place + 1), launch, phase, piece, devices)
    for shift, held in enumerate(onward(piece, points), 1):
        result = forward_plain(scalar(place + 1 - shift), result, phase, held, devices)
    return result[None]


def quarters(devices):
    part = devices // 8
    return [tuple(range(at * part, (at + 1) * part)) for at in range(4)]


def chips_of(devices):
    near, close, middle, far = quarters(devices)
    return [near] + [middle] + [close] + [(chip,) for chip in far]


def groups_of(devices):
    return [
        tuple(2 * chip + core for chip in chips for core in range(2))
        for chips in chips_of(devices)
    ]


def on_device(devices, points, launch, phase, profiles, weights):
    _, modes, _ = launch.shape
    if not regular(modes, devices):
        return on_device_plain(devices, points, launch, phase, profiles, weights)
    place = lax.axis_index("gz")
    me = lax.axis_index("modes")
    here = scalar(me, jnp.int32)
    fields = inverse(scalar(place + 1), launch, phase, devices)
    fields = lax.all_to_all(fields, "modes", 0, 0, tiled=True)
    sent = kerr(here, fields, profiles, profiles.T, weights[None, :], modes)
    chips = devices // 2
    keeps, (near, far) = sent[:chips], sent[chips:]
    swap = [(a, a ^ 1) for a in range(devices)]
    far = lax.ppermute(far, "modes", swap)
    near = lax.ppermute(near, "modes", swap)
    got = [jnp.stack([keeps[0], near[0]])]
    got += pack(keeps[1 : chips // 2], near) + pack(keeps[chips // 2 :], far)
    for chip in range(1, chips):
        pairs = [(a, a ^ (2 * chip)) for a in range(devices)]
        got[chip] = lax.ppermute(got[chip], "modes", pairs)
    waiting = []
    for group in chips_of(devices):
        pieces = jnp.concatenate([got[chip] for chip in group], 0)
        waiting.append([pieces] + onward(pieces, points))
    result = launch
    for shift in range(points):
        last = shift == points - 1
        result, *ahead = late(
            here,
            scalar(place + 1 - shift),
            [held[shift] for held in waiting],
            result,
            turn if shift == 1 else phase,
            devices,
            shift != 1,
            last,
        )
        if ahead:
            turn = ahead[0]
    return result[None]


def solution(mesh):
    in_specs = (P(None, "modes", None), P("modes", None), P(), P())
    out_specs = P("gz", None, "modes", None)
    devices, points = mesh.shape["modes"], mesh.shape["gz"]
    body = functools.partial(on_device, devices, points)
    return jax.shard_map(body, mesh=mesh, in_specs=in_specs, out_specs=out_specs, check_vma=False)
```

```python
import functools
import math

import jax
import jax.numpy as jnp
import numpy as np
from jax import lax
from jax.experimental import pallas as pl
from jax.experimental.pallas import tpu as pltpu
from jax.sharding import PartitionSpec as P

RADIX = 128
STRIPES = 8
HALVES = 4
KSTEP = 256
KTILE = 512
SPACES = pltpu.MemorySpace

f32 = jnp.float32
bf16 = jnp.bfloat16


def halves(table):
    high = table.astype(jnp.bfloat16)
    low = (table - high.astype(np.float64)).astype(jnp.bfloat16)
    return high, low


@functools.lru_cache(None)
def tables(length):
    radix = RADIX
    other = length // radix
    index = np.arange(radix)
    second = np.arange(other)
    scale = 1.0 / math.sqrt(length)
    angle = 2.0 * math.pi / radix * (index[:, None] * index[None, :] % radix)
    cos, sin = np.cos(angle), np.sin(angle)
    last = 2.0 * math.pi / other * (second[:, None] * second[None, :] % other)
    cos2, sin2 = np.cos(last), np.sin(last)
    turn = 2.0 * math.pi / length * (index[:, None] * second[None, :] % length)
    twist = np.stack([np.cos(turn), np.sin(turn)]).astype(np.float32)
    inv_first = np.block([[cos, -sin], [sin, cos]])
    inv_second = np.block([[cos2, sin2], [-sin2, cos2]]) * scale
    fwd_first = np.block([[sin2, cos2], [-cos2, sin2]])
    fwd_second = np.block([[cos, sin], [-sin, cos]]) * scale
    return dict(
        twist=twist,
        inv_first=halves(inv_first),
        inv_second=halves(inv_second),
        fwd_first=halves(fwd_first),
        fwd_second=halves(fwd_second),
    )


def split(values):
    high = values.astype(bf16)
    return high, (values - high.astype(f32)).astype(bf16)


def dot(left, right):
    return lax.dot_general(left, right, (((1,), (0,)), ((), ())), preferred_element_type=f32)


TWO_PI = 2.0 * math.pi
TWO_PI_HIGH = float(np.float32(6.28125))
TWO_PI_LOW = TWO_PI - TWO_PI_HIGH
SIN_TERMS = [(-1) ** n / math.factorial(2 * n + 1) for n in range(6)]
COS_TERMS = [(-1) ** n / math.factorial(2 * n) for n in range(7)]


def sincos(phase):
    turns = jnp.round(phase * (1.0 / TWO_PI))
    rest = (phase - turns * TWO_PI_HIGH) - turns * TWO_PI_LOW
    half = 0.5 * rest
    square = half * half
    sine = SIN_TERMS[-1]
    for term in SIN_TERMS[-2::-1]:
        sine = sine * square + term
    sine = sine * half
    cosine = COS_TERMS[-1]
    for term in COS_TERMS[-2::-1]:
        cosine = cosine * square + term
    twice = sine + sine
    return twice * cosine, 1.0 - twice * sine


def specs(text):
    spaces = dict(s=SPACES.SMEM, v=SPACES.VMEM, h=SPACES.HBM, a=pl.ANY)
    return [pl.BlockSpec(memory_space=spaces[letter]) for letter in text]


def params():
    return pltpu.CompilerParams(vmem_limit_bytes=48 * 1024 * 1024)


def stripe(at, length):
    width = length // STRIPES
    return slice(at * width, (at + 1) * width)


def inverse_kernel(modes, devices, factor, launch, phase, *rest):
    tables_in, out, natural, turned, launched, phases = rest[:5], *rest[5:10]
    tables_here, sems, table_sems = rest[10:15], rest[15], rest[16]
    radix = RADIX
    length = launch.shape[-1]
    half = modes // 2
    copies = []
    for side in range(2):
        rows = slice(side * half, (side + 1) * half)
        for at in range(HALVES):
            width = length // HALVES
            cut = slice(at * width, (at + 1) * width)
            sem = 2 * (side * HALVES + at)
            copies.append(
                [
                    pltpu.make_async_copy(
                        launch.at[:, rows, cut], launched.at[:, rows, cut], sems.at[sem]
                    ),
                    pltpu.make_async_copy(
                        phase.at[rows, cut], phases.at[rows, cut], sems.at[sem + 1]
                    ),
                ]
            )
            for copy in copies[-1]:
                copy.start()
        if side == 0:
            more = [
                pltpu.make_async_copy(there, here, table_sems.at[at])
                for at, (there, here) in enumerate(zip(tables_in, tables_here))
            ]
            for copy in more:
                copy.start()
    twist, fh, fl, sh, sl = tables_here
    for side in range(2):

        def rotate(k1, carry, side=side):
            at = pl.ds(pl.multiple_of(k1 * radix, radix), radix)
            rows = pl.ds(pl.multiple_of(k1 * half, half), half)
            mine = slice(side * half, (side + 1) * half)
            sine, cosine = sincos(phases[mine, at] * factor[0, 0])
            real, imag = launched[0, mine, at], launched[1, mine, at]
            natural[0, rows, :] = real * cosine - imag * sine
            natural[1, rows, :] = real * sine + imag * cosine
            return carry

        for at in range(HALVES):
            for copy in copies[side * HALVES + at]:
                copy.wait()
            part = radix // HALVES
            lax.fori_loop(at * part, (at + 1) * part, rotate, 0, unroll=16)
        if side == 0:
            for copy in more:
                copy.wait()
        for pair in range(half // 2):
            both = []
            for m in (2 * pair, 2 * pair + 1):
                both.append(
                    jnp.concatenate(
                        [natural[c, pl.ds(m, radix, stride=half), :] for c in range(2)], 0
                    )
                )
            high, low = split(jnp.concatenate(both, 1))
            section = dot(fh[...], high) + (dot(fh[...], low) + dot(fl[...], high))
            rows = []
            for one in range(2):
                real = section[:radix, one * radix : (one + 1) * radix]
                imag = section[radix:, one * radix : (one + 1) * radix]
                rows.append(
                    jnp.concatenate(
                        [real * twist[0] - imag * twist[1], real * twist[1] + imag * twist[0]], 1
                    )
                )
            high, low = split(jnp.concatenate(rows, 0))
            final = dot(high, sh[...]) + (dot(low, sh[...]) + dot(high, sl[...]))
            for one in range(2):
                m = side * half + 2 * pair + one
                for c in range(2):
                    turned[c, pl.ds(m, radix, stride=modes), :] = final[
                        one * radix : (one + 1) * radix, c * radix : (c + 1) * radix
                    ]
    each = radix // devices
    for t2 in range(radix):
        target, slot = divmod(t2, each)
        for c in range(2):
            out[target, c * modes : (c + 1) * modes, slot * radix : (slot + 1) * radix] = turned[
                c, t2 * modes : (t2 + 1) * modes, :
            ].astype(bf16)


def inverse(factor, launch, phase, devices):
    _, modes, length = launch.shape
    table = tables(length)
    held = [table["twist"], *table["inv_first"], *table["inv_second"]]
    return pl.pallas_call(
        functools.partial(inverse_kernel, modes, devices),
        out_shape=jax.ShapeDtypeStruct((devices, 2 * modes, length // devices), bf16),
        in_specs=specs("shhhhhhh"),
        out_specs=specs("v")[0],
        scratch_shapes=[
            pltpu.VMEM((2, RADIX * modes // 2, RADIX), f32),
            pltpu.VMEM((2, RADIX * modes, RADIX), f32),
            pltpu.VMEM(launch.shape, f32),
            pltpu.VMEM(phase.shape, f32),
            *[pltpu.VMEM(value.shape, value.dtype) for value in held],
            pltpu.SemaphoreType.DMA((4 * HALVES,)),
            pltpu.SemaphoreType.DMA((len(held),)),
        ],
        compiler_params=params(),
        name="inverse",
    )(
        factor,
        *[
            pltpu.with_memory_space_constraint(value, SPACES.HBM)
            for value in (launch, phase, *map(jnp.asarray, held))
        ],
    )


def kerr_kernel(modes, devices, step, lanes, me, fields, profiles, flipped, weights, *rest):
    chips = devices // 2
    keeps, gives = rest[:chips], rest[chips : chips + 2]
    fields_t, total_t, total = rest[chips + 2 :]
    points = profiles.shape[0]
    width = fields.shape[-1]
    tiles = width // lanes
    for tile in range(tiles):
        cut = slice(tile * lanes, (tile + 1) * lanes)
        for c in range(2):
            rows = slice(c * modes, (c + 1) * modes)
            block = jnp.concatenate([fields[source, rows, cut] for source in range(devices)], 0)
            fields_t[c, cut, :] = block.T
    for at in range(0, points, step):
        these = slice(at, at + step)
        for tile in range(tiles):
            cut = slice(tile * lanes, (tile + 1) * lanes)
            real = dot(fields_t[0, cut, :], flipped[:, these])
            imag = dot(fields_t[1, cut, :], flipped[:, these])
            power = weights[:, these] * (real * real + imag * imag)
            parts = [
                dot((power * real).astype(bf16), profiles[these, :]),
                dot((power * imag).astype(bf16), profiles[these, :]),
            ]
            if at == 0:
                total_t[0, cut, :], total_t[1, cut, :] = parts
            else:
                total_t[0, cut, :] += parts[0]
                total_t[1, cut, :] += parts[1]
    for c in range(2):
        for tile in range(width // RADIX):
            cut = slice(tile * RADIX, (tile + 1) * RADIX)
            total[c, :, cut] = total_t[c, cut, :].T
    for hop in range(devices):
        rows = pl.ds(pl.multiple_of((me[0, 0] ^ hop) * modes, modes), modes)
        chip, other = divmod(hop, 2)
        target = gives[chip // (chips // 2)].at[chip % (chips // 2)] if other else keeps[chip]
        for c in range(2):
            target[c * modes : (c + 1) * modes, :] = total[c, rows, :].astype(bf16)


def kerr(me, fields, profiles, flipped, weights, modes):
    devices, _, width = fields.shape
    chips = devices // 2
    return pl.pallas_call(
        functools.partial(kerr_kernel, modes, devices, KSTEP, KTILE),
        out_shape=[jax.ShapeDtypeStruct((2 * modes, width), bf16)] * chips
        + [jax.ShapeDtypeStruct((chips // 2, 2 * modes, width), bf16)] * 2,
        in_specs=specs("svvvv"),
        out_specs=specs("v" * (chips + 2)),
        scratch_shapes=[
            pltpu.VMEM((2, width, devices * modes), bf16),
            pltpu.VMEM((2, width, devices * modes), f32),
            pltpu.VMEM((2, devices * modes, width), f32),
        ],
        compiler_params=params(),
        name="kerr",
    )(me, fields, profiles, flipped, weights)


def pack_kernel(count, *refs):
    keeps, got, outs = refs[:count], refs[count], refs[count + 1 :]
    skip = got.shape[0] - count
    for at in range(count):
        outs[at][0] = keeps[at][...]
        outs[at][1] = got[skip + at]


def pack(keeps, got):
    count = len(keeps)
    return pl.pallas_call(
        functools.partial(pack_kernel, count),
        out_shape=[jax.ShapeDtypeStruct((2,) + keeps[0].shape, bf16)] * count,
        in_specs=specs("v" * (count + 1)),
        out_specs=specs("v" * count),
        compiler_params=params(),
        name="pack",
    )(*keeps, got)


def first_section(modes, block, source, each, twist, fh, fl, write):
    radix = RADIX
    rows = []
    for slot in range(each):
        at = slice(slot * radix, (slot + 1) * radix)
        rows.append(
            jnp.concatenate([block[c * modes : (c + 1) * modes, at] for c in range(2)], 1)
        )
    block = jnp.concatenate(rows, 0)
    section = dot(block, fh[...]) + dot(block, fl[...])
    for slot in range(each):
        here = slice(slot * modes, (slot + 1) * modes)
        real, imag = section[here, :radix], section[here, radix:]
        row = pl.ds(source * each + slot, 1)
        cosine, sine = twist[0, row, :], twist[1, row, :]
        write(0, slot, real * cosine + imag * sine)
        write(1, slot, imag * cosine - real * sine)


def late_kernel(modes, devices, first, alone, last, me, factor, base, phase, *rest):
    (twist, fh, fl, sh, sl), rest = rest[:5], rest[5:]
    count = len(groups_of(devices))
    groups, out, rest = rest[:count], rest[count], rest[count + 1 :]
    if not alone:
        ahead, rest = rest[0], rest[1:]
    turned, final = rest[:2]
    spare = rest[2:]
    length = base.shape[-1]
    inward = []
    if not first:
        *spare, turns, arrive = spare
        for at in range(STRIPES):
            cut = stripe(at, length)
            inward.append(
                pltpu.make_async_copy(phase.at[:, :, cut], turns.at[:, :, cut], arrive.at[at])
            )
            inward[-1].start()
    radix = RADIX
    each = radix // devices
    size = each * modes
    length = base.shape[-1]
    for group, hops in zip(groups, groups_of(devices)):
        for at, hop in enumerate(hops):
            source = me[0, 0] ^ hop

            def write(c, slot, values, source=source):
                rows = pl.ds(pl.multiple_of(source * size + slot * modes, modes), modes)
                turned[c, rows, :] = values

            first_section(modes, group.at[at], source, each, twist, fh, fl, write)
    for pair in range(modes // 2):
        both = []
        for m in (2 * pair, 2 * pair + 1):
            both.append(
                jnp.concatenate([turned[c, pl.ds(m, radix, stride=modes), :] for c in range(2)], 0)
            )
        high, low = split(jnp.concatenate(both, 1))
        section = dot(sh[...], high) + (dot(sh[...], low) + dot(sl[...], high))
        for side in range(2):
            for c in range(2):
                final[c, pl.ds(2 * pair + side, radix, stride=modes), :] = section[
                    c * radix : (c + 1) * radix, side * radix : (side + 1) * radix
                ]
    result = spare[0] if last else out

    def finish(k1, carry):
        at = pl.ds(pl.multiple_of(k1 * radix, radix), radix)
        rows = pl.ds(pl.multiple_of(k1 * modes, modes), modes)
        if first:
            sine, cosine = sincos(phase[:, at] * factor[0, 0])
        else:
            sine, cosine = turns[0, :, at], turns[1, :, at]
        if not alone:
            ahead[0, :, at], ahead[1, :, at] = sincos(phase[:, at] * (factor[0, 0] - 1.0))
        real, imag = final[0, rows, :], final[1, rows, :]
        result[0, :, at] = base[0, :, at] + (real * cosine + imag * sine)
        result[1, :, at] = base[1, :, at] + (imag * cosine - real * sine)
        return carry

    copies = []
    for at in range(STRIPES):
        cut = stripe(at, length)
        part = radix // STRIPES
        if not first:
            inward[at].wait()
        lax.fori_loop(at * part, (at + 1) * part, finish, 0, unroll=8)
        if last:
            copies.append(
                pltpu.make_async_copy(result.at[:, :, cut], out.at[:, :, cut], spare[1].at[at])
            )
            copies[-1].start()
    for copy in copies:
        copy.wait()


def late(me, factor, groups, base, phase, devices, first, last):
    _, modes, length = base.shape
    ahead = first and not last
    table = tables(length)
    spare = [pltpu.VMEM(base.shape, f32), pltpu.SemaphoreType.DMA((STRIPES,))]
    spare = spare * last + spare * (not first)
    if not first:
        phase = pltpu.with_memory_space_constraint(phase, SPACES.HBM)
    return pl.pallas_call(
        functools.partial(late_kernel, modes, devices, first, not ahead, last),
        out_shape=[jax.ShapeDtypeStruct(base.shape, f32)] * (2 if ahead else 1),
        in_specs=specs("ssv" + ("v" if first else "h") + "vvvvv" + "v" * len(groups)),
        out_specs=specs("vv" if ahead else "h" if last else "v"),
        scratch_shapes=[pltpu.VMEM((2, RADIX * modes, RADIX), f32)] * 2 + spare,
        compiler_params=params(),
        name="late",
    )(
        me,
        factor,
        base,
        phase,
        table["twist"],
        *table["fwd_first"],
        *table["fwd_second"],
        *groups,
    )


def regular(modes, devices):
    return modes % 16 == 0 and devices & (devices - 1) == 0 and 8 <= devices <= RADIX


def matrix(name, length):
    high, low = tables(length)[name]
    return high.astype(np.float32) + low.astype(np.float32)


def einsum(text, left, right):
    return jnp.einsum(text, left, right, precision=lax.Precision.HIGHEST)


def inverse_plain(factor, launch, phase, devices):
    _, modes, length = launch.shape
    twist = tables(length)["twist"]
    angle = phase * factor[0, 0]
    cosine, sine = jnp.cos(angle), jnp.sin(angle)
    real = launch[0] * cosine - launch[1] * sine
    imag = launch[0] * sine + launch[1] * cosine
    both = jnp.stack([real, imag]).reshape(2, modes, RADIX, -1)
    first = matrix("inv_first", length).reshape(2, RADIX, 2, RADIX)
    real, imag = einsum("dtck,cmkj->dmtj", first, both)
    both = jnp.stack([real * twist[0] - imag * twist[1], real * twist[1] + imag * twist[0]])
    other = length // RADIX
    second = matrix("inv_second", length).reshape(2, other, 2, other)
    both = einsum("cmtj,cjdu->dmtu", both, second).astype(bf16)
    both = both.reshape(2, modes, devices, -1)
    return both.transpose(2, 0, 1, 3).reshape(devices, 2 * modes, -1)


def kerr_plain(fields, profiles, weights, modes):
    devices, _, width = fields.shape
    fields = fields.reshape(devices, 2, modes, width).swapaxes(0, 1)
    fields = fields.reshape(2, devices * modes, width)
    expanded = jnp.einsum("pm,cmt->cpt", profiles, fields, preferred_element_type=f32)
    power = weights * (expanded[0] * expanded[0] + expanded[1] * expanded[1])
    cubed = (power * expanded).astype(bf16)
    projected = jnp.einsum("pm,cpt->cmt", profiles, cubed, preferred_element_type=f32)
    projected = projected.astype(bf16).reshape(2, devices, modes, width)
    return projected.swapaxes(0, 1).reshape(devices, 2 * modes, width)


def forward_plain(factor, base, phase, piece, devices):
    _, modes, length = base.shape
    other = length // RADIX
    twist = tables(length)["twist"]
    both = piece.astype(f32).reshape(devices, 2, modes, -1, other)
    both = both.transpose(1, 2, 0, 3, 4).reshape(2, modes, RADIX, other)
    first = matrix("fwd_first", length).reshape(2, other, 2, other)
    real, imag = einsum("cmtu,cudj->dmtj", both, first)
    both = jnp.stack([real * twist[0] + imag * twist[1], imag * twist[0] - real * twist[1]])
    second = matrix("fwd_second", length).reshape(2, RADIX, 2, RADIX)
    real, imag = einsum("dkct,cmtj->dmkj", second, both).reshape(2, modes, length)
    angle = phase * factor[0, 0]
    cosine, sine = jnp.cos(angle), jnp.sin(angle)
    return base + jnp.stack([real * cosine + imag * sine, imag * cosine - real * sine])


def scalar(value, dtype=f32):
    return value.astype(dtype).reshape(1, 1)


def onward(values, points):
    held = []
    for shift in range(1, points):
        pairs = [(k, k + shift) for k in range(points - shift)]
        held.append(lax.ppermute(values, "gz", pairs))
    return held


def on_device_plain(devices, points, launch, phase, profiles, weights):
    _, modes, _ = launch.shape
    place = lax.axis_index("gz")
    exchange = functools.partial(
        lax.all_to_all, axis_name="modes", split_axis=0, concat_axis=0, tiled=True
    )
    piece = exchange(inverse_plain(scalar(place + 1), launch, phase, devices))
    piece = exchange(kerr_plain(piece, profiles, weights[:, None], modes))
    result = forward_plain(scalar(place + 1), launch, phase, piece, devices)
    for shift, held in enumerate(onward(piece, points), 1):
        result = forward_plain(scalar(place + 1 - shift), result, phase, held, devices)
    return result[None]


def quarters(devices):
    part = devices // 8
    return [tuple(range(at * part, (at + 1) * part)) for at in range(4)]


def chips_of(devices):
    near, close, middle, far = quarters(devices)
    return [near] + [middle] + [close] + [(chip,) for chip in far]


def groups_of(devices):
    return [
        tuple(2 * chip + core for chip in chips for core in range(2))
        for chips in chips_of(devices)
    ]


def on_device(devices, points, launch, phase, profiles, weights):
    _, modes, _ = launch.shape
    if not regular(modes, devices):
        return on_device_plain(devices, points, launch, phase, profiles, weights)
    place = lax.axis_index("gz")
    me = lax.axis_index("modes")
    here = scalar(me, jnp.int32)
    fields = inverse(scalar(place + 1), launch, phase, devices)
    fields = lax.all_to_all(fields, "modes", 0, 0, tiled=True)
    sent = kerr(here, fields, profiles, profiles.T, weights[None, :], modes)
    chips = devices // 2
    keeps, (near, far) = sent[:chips], sent[chips:]
    swap = [(a, a ^ 1) for a in range(devices)]
    far = lax.ppermute(far, "modes", swap)
    near = lax.ppermute(near, "modes", swap)
    got = [jnp.stack([keeps[0], near[0]])]
    got += pack(keeps[1 : chips // 2], near) + pack(keeps[chips // 2 :], far)
    for chip in range(1, chips):
        pairs = [(a, a ^ (2 * chip)) for a in range(devices)]
        got[chip] = lax.ppermute(got[chip], "modes", pairs)
    waiting = []
    for group in chips_of(devices):
        pieces = jnp.concatenate([got[chip] for chip in group], 0)
        waiting.append([pieces] + onward(pieces, points))
    result = launch
    for shift in range(points):
        last = shift == points - 1
        result, *ahead = late(
            here,
            scalar(place + 1 - shift),
            [held[shift] for held in waiting],
            result,
            turn if shift == 1 else phase,
            devices,
            shift != 1,
            last,
        )
        if ahead:
            turn = ahead[0]
    return result[None]


def solution(mesh):
    in_specs = (P(None, "modes", None), P("modes", None), P(), P())
    out_specs = P("gz", None, "modes", None)
    devices, points = mesh.shape["modes"], mesh.shape["gz"]
    body = functools.partial(on_device, devices, points)
    return jax.shard_map(body, mesh=mesh, in_specs=in_specs, out_specs=out_specs, check_vma=False)
```
